32 devices in a mesh: gx: 4 (over y, x), gy: 8 (over z, core).
Axes of the slice: x: 2, y: 2, z: 4, core: 2. Of those that a mesh axis runs over, the one named last changes fastest.
Arguments:
- populations: float32 [19, 128, 64, 256], P(None, 'gx', 'gy'), may hold values from 0.02 to 0.08
- mass: float32 [256, 1024], P('gx', 'gy'), may hold values from 0.2 to 1
- modulus: float32 [256, 1024], P('gx', 'gy'), may hold values from 0.1 to 0.5
- cell_live: int32 [256, 1024], P('gx', 'gy'), may hold values 0 or 1
- stiff_ref: float32 [12, 12], replicated, as said below
- rec_block: int32 [131072], P(('gx', 'gy')), may hold values from 0 to 255
- rec_owner: int32 [131072, 1], P(('gx', 'gy')), may hold values from 0 to 31; in each aligned block of 4096 rows (0 to 4095, 4096 to 8191, ...) at most 256 rows name the same one
- rec_node: int32 [131072], P(('gx', 'gy')), may hold values from 0 to 8191
- rbf_weight: float32 [131072, 256], P(('gx', 'gy')), may hold values from 0 to 2
Outputs:
- populations_next: float32 [19, 128, 64, 256], P(None, 'gx', 'gy')
- displacement: float32 [3, 256, 1024], P(None, 'gx', 'gy')
The draws below stay inside these ranges and needn't reach their ends.
Inputs may be any that keep to these rules, and one draw needn't show every extreme that they name: `rec_owner`: in the records of one device no owner is named more than 256 times, and every owner is named by some record. `stiff_ref`: symmetric with a positive diagonal that exceeds the sum of magnitudes of each row's other entries.
All inputs are finite; a program needn't handle non-finite values. No bound on the sum of `cell_live` on one device may be relied on, other than what follows from the above.
Results may differ from the reference program's by a relative error of at most 0.0003.
Values sent between devices are 32-bit elements; how exact they have to be, the bound alone decides.
A program may use at most 128 MiB of HBM per device.

```python
import math
import jax
import jax.numpy as jnp
import numpy as np
from jax import lax

CX = 32
CY = 8
CZ = 256
PU = 64
PV = 128
R_DEV = 4096
ITERS = 2
NX = 128
NY = 64
NZ = 256
NU = 256
NV = 1024
CAP = 256
R_TOTAL = 131072
N_GX = 4
N_GY = 8
DEVICES = 32


def draw_stiff_ref(key, part):
    first_key, second_key = jax.random.split(jax.random.fold_in(key, 17))
    offdiag = jax.random.uniform(first_key, (12, 12), jnp.float32, -0.3, 0.3)
    offdiag = (offdiag + offdiag.T) * 0.5 * (1.0 - jnp.eye(12, dtype=jnp.float32))
    diagonal = jnp.sum(jnp.abs(offdiag), axis=1) + jax.random.uniform(second_key, (12,), jnp.float32, 0.3, 0.8)
    return offdiag + jnp.diag(diagonal)


def plant(values, rng, smallest, top_value):
    extent = values.shape
    index_at = [jax.random.randint(jax.random.fold_in(rng, axis), (), 0, extent[axis]) for axis in range(len(extent))]
    values = values.at[tuple(index_at)].set(smallest)
    longest = extent.index(max(extent))
    index_at[longest] = (index_at[longest] + 1) % extent[longest]
    return values.at[tuple(index_at)].set(top_value)


def steps_of(stream_key, extent, pieces, low, high):
    gain = 1.0
    for axis_at, parts in pieces:
        draws = jax.random.uniform(jax.random.fold_in(jax.random.fold_in(stream_key, 6), axis_at), (parts,), jnp.float32, low / len(pieces), high / len(pieces))
        gain = gain * jnp.repeat(jnp.exp(draws), extent[axis_at] // parts).reshape((-1,) + (1,) * (len(extent) - 1 - axis_at))
    return gain


def deal_out(own_key, own, number, rows, number_of, top, bound, slope):
    order = jax.random.permutation(own_key, number_of)
    crowded, common = portions_of(number_of, rows * top, bound, slope, True), portions_of(number_of, rows * top, bound, slope, False)
    places = jnp.arange(number_of)

    def named(tallies, rotation):
        used = int((tallies > 0).sum())
        fixed = max(1, used // 4)
        moved = fixed + (places - fixed + rotation * (used - fixed)) % max(1, number_of - fixed)
        return jnp.zeros((number_of,), jnp.int32).at[order[jnp.where(places < fixed, places, moved)]].set(jnp.asarray(tallies, jnp.int32))

    tallies = jnp.where(number % 4 == 0, named(crowded, number // 4), named(common, number - number // 4 - 1))
    mixed = jax.random.permutation(jax.random.fold_in(own, 3), number_of)
    donor, taker = mixed[0:number_of // 2 * 2:2], mixed[1:number_of // 2 * 2:2]
    slack = jnp.minimum(tallies[donor] - 1, bound - tallies[taker]) // 2
    slack = jnp.where((donor == order[0]) | (taker == order[0]) | (tallies[taker] == 0), 0, jnp.maximum(slack, 0))
    moved = jax.random.randint(jax.random.fold_in(own, 4), (number_of // 2,), 0, 1 << 20) % (slack + 1)
    tallies = tallies.at[donor].add(-moved).at[taker].add(moved)
    members = jnp.searchsorted(jnp.cumsum(tallies), jnp.arange(rows * top), side="right").astype(jnp.int32)
    grid = members.reshape(top, rows).T
    grid = grid[jax.random.permutation(jax.random.fold_in(own, 1), rows)]
    rotation = jax.random.randint(jax.random.fold_in(own, 2), (rows, 1), 0, top)
    return jnp.take_along_axis(grid, (jnp.arange(top)[None, :] + rotation) % top, axis=1)


def portions_of(amount, total, reach, lean, full):
    portions = [(1 << 20) // math.isqrt(standing ** lean) + 1 for standing in range(1, amount + 1)]
    largest = reach if full else min(reach, max(-(-total // amount), total * portions[0] // sum(portions)))
    least = 1 if total - largest >= amount - 1 else 0
    holding, rest = [largest] + [least] * (amount - 1), total - largest - least * (amount - 1)
    while rest > 0:
        movable = [i for i in range(1, amount) if holding[i] < largest] or [i for i in range(1, amount) if holding[i] < reach]
        pool, budget = sum([portions[i] for i in movable]), rest
        for i in movable:
            extra = min(reach - holding[i], max(1, budget * portions[i] // pool), rest)
            holding[i] = holding[i] + extra
            rest = rest - extra
    return np.array(holding)


def setup_inputs(seed: int = 0) -> dict:
    seeds = jax.random.split(jax.random.key(seed), 10)
    populations = jnp.clip(0.02 + 0.06 * jax.random.uniform(seeds[0], (19, NX, NY, NZ), jnp.float32) ** steps_of(seeds[0], (19, NX, NY, NZ), ((1, 4), (2, 8)), -0.2, 0.2), 0.02, 0.08)
    mass = jnp.clip(jnp.exp(math.log(1.0) - 1.609438 * jax.random.uniform(seeds[1], (NU, NV), jnp.float32) ** steps_of(seeds[1], (NU, NV), ((0, 4), (1, 8)), -0.2, 0.2)), 0.2, 1.0)
    modulus = jnp.clip(jnp.exp(math.log(0.5) - 1.609438 * jax.random.uniform(seeds[2], (NU, NV), jnp.float32) ** steps_of(seeds[2], (NU, NV), ((0, 4), (1, 8)), -0.2, 0.2)), 0.1, 0.5)
    cell_live = plant((jax.random.randint(seeds[3], (NU, NV), 0, 8) < 7).astype(jnp.int32), jax.random.fold_in(seeds[3], 1), 0, 1)
    stiff_ref = draw_stiff_ref(jax.random.fold_in(seeds[9], 71), 0)
    rec_block = plant(jax.random.randint(seeds[5], (R_TOTAL,), 0, CX * CY), jax.random.fold_in(seeds[5], 1), 0, (CX * CY) - 1).astype(jnp.int32)
    rec_owner_keys = jax.random.split(jax.random.fold_in(seeds[6], 1), R_TOTAL // R_DEV)
    rec_owner_turns = jax.random.permutation(jax.random.fold_in(seeds[6], 3), R_TOTAL // R_DEV)
    rec_owner = jax.vmap(lambda own, number: deal_out(jax.random.fold_in(seeds[6], 2), own, number, R_DEV, DEVICES, 1, CAP, 2))(rec_owner_keys, rec_owner_turns).reshape((R_TOTAL, 1))
    rec_node = plant(jax.random.randint(seeds[7], (R_TOTAL,), 0, PU * PV), jax.random.fold_in(seeds[7], 1), 0, (PU * PV) - 1).astype(jnp.int32)
    rbf_weight = jnp.clip(2.0 * jax.random.uniform(seeds[8], (R_TOTAL, CZ), jnp.float32) ** steps_of(seeds[8], (R_TOTAL, CZ), ((0, 32),), -0.2, 0.2), 0.0, 2.0)
    return {"populations": populations, "mass": mass, "modulus": modulus, "cell_live": cell_live, "stiff_ref": stiff_ref, "rec_block": rec_block, "rec_owner": rec_owner, "rec_node": rec_node, "rbf_weight": rbf_weight}


lattice_dirs = ((0, 0, 0), (1, 0, 0), (-1, 0, 0), (0, 1, 0), (0, -1, 0), (0, 0, 1), (0, 0, -1),
                (1, 1, 0), (-1, -1, 0), (1, -1, 0), (-1, 1, 0), (1, 0, 1), (-1, 0, -1), (1, 0, -1),
                (-1, 0, 1), (0, 1, 1), (0, -1, -1), (0, 1, -1), (0, -1, 1))
lattice_weights = (1.0 / 3.0,) + (1.0 / 18.0,) * 6 + (1.0 / 36.0,) * 12
relax_rate = 1.25
coupling = 0.1


def combine_dirs(fields, direction):
    total = None
    for axis_pos in range(3):
        if direction[axis_pos] != 0:
            term = direction[axis_pos] * fields[axis_pos]
            total = term if total is None else total + term
    return total


def collide(populations):
    density = populations[0]
    for number in range(1, 19):
        density = density + populations[number]
    moment = []
    for axis_pos in range(3):
        total = None
        for number in range(19):
            if lattice_dirs[number][axis_pos] != 0:
                term = lattice_dirs[number][axis_pos] * populations[number]
                total = term if total is None else total + term
        moment.append(total)
    velocity = [moment[axis_pos] / density for axis_pos in range(3)]
    squared = velocity[0] * velocity[0] + velocity[1] * velocity[1] + velocity[2] * velocity[2]
    relaxed = []
    for number in range(19):
        projected = combine_dirs(velocity, lattice_dirs[number])
        if projected is None:
            bracket = 1.0 - 1.5 * squared
        else:
            bracket = 1.0 + 3.0 * projected + 4.5 * projected * projected - 1.5 * squared
        equilibrium = lattice_weights[number] * density * bracket
        relaxed.append(populations[number] - relax_rate * (populations[number] - equilibrium))
    return jnp.stack(relaxed), jnp.stack(moment)


def apply_forcing(read, forcing):
    result = []
    for number in range(19):
        projected = combine_dirs(forcing, lattice_dirs[number])
        if projected is None:
            result.append(read[number])
        else:
            result.append(read[number] + 3.0 * lattice_weights[number] * projected)
    return jnp.stack(result)


def stiffness(field, scale, stiff_ref):
    corners = jnp.concatenate([field, jnp.roll(field, -1, 1), jnp.roll(field, -1, 2),
                               jnp.roll(jnp.roll(field, -1, 1), -1, 2)], 0)
    result = scale[None] * jnp.einsum('kl,lab->kab', stiff_ref, corners, precision=lax.Precision.HIGHEST)
    return (result[0:3] + jnp.roll(result[3:6], 1, 1) + jnp.roll(result[6:9], 1, 2)
            + jnp.roll(jnp.roll(result[9:12], 1, 1), 1, 2))


def reference(populations, mass, modulus, cell_live, stiff_ref, rec_block, rec_owner, rec_node, rbf_weight):
    relaxed, moment = collide(populations)
    read = jnp.stack([jnp.roll(relaxed[number], lattice_dirs[number], axis=(0, 1, 2)) for number in range(19)])
    blocks_all = moment.reshape(3, N_GX, CX, N_GY, CY, NZ).transpose(1, 3, 0, 2, 4, 5).reshape(DEVICES, 3, CX * CY, NZ)
    block_dev = rec_block.reshape(DEVICES, R_DEV)
    kernel_dev = rbf_weight.reshape(DEVICES, R_DEV, CZ)

    def interpolate(packed):
        blocks, chosen, kernel = packed
        picked = blocks[:, chosen, :]
        return jnp.sum(picked * kernel[None], axis=2)

    loads = lax.map(interpolate, (blocks_all, block_dev, kernel_dev))
    loads_flat = loads.transpose(1, 0, 2).reshape(3, R_TOTAL)
    owners = rec_owner[:, 0]
    owner_x = owners // N_GY
    owner_y = owners % N_GY
    target = (owner_x * PU + rec_node // PV) * NV + owner_y * PV + rec_node % PV
    force = jax.ops.segment_sum(loads_flat.T, target, num_segments=NU * NV).T.reshape(3, NU, NV)
    scale = cell_live.astype(jnp.float32) * (modulus + jnp.roll(modulus, -1, 0) + jnp.roll(modulus, -1, 1)
                                             + jnp.roll(jnp.roll(modulus, -1, 0), -1, 1)) * 0.25

    def operate(field):
        return mass[None] * field + stiffness(field, scale, stiff_ref)

    displacement = jnp.zeros((3, NU, NV), jnp.float32)
    residual = force
    direction = force
    norm_now = jnp.sum(residual * residual)
    for step in range(ITERS):
        image = operate(direction)
        step_size = norm_now / jnp.sum(direction * image)
        displacement = displacement + step_size * direction
        residual = residual - step_size * image
        if step + 1 < ITERS:
            norm_next = jnp.sum(residual * residual)
            direction = residual + (norm_next / norm_now) * direction
            norm_now = norm_next
    moved = displacement.reshape(3, NU * NV)[:, target]
    moved_dev = moved.reshape(3, DEVICES, R_DEV).transpose(1, 0, 2)

    def spread(packed):
        chosen, kernel, shifted = packed
        empty = jnp.zeros((3, CX * CY, CZ), jnp.float32)
        return empty.at[:, chosen, :].add(coupling * kernel[None] * shifted[:, :, None])

    forcing = lax.map(spread, (block_dev, kernel_dev, moved_dev))
    forcing = forcing.reshape(N_GX, N_GY, 3, CX, CY, NZ).transpose(2, 0, 3, 1, 4, 5).reshape(3, NX, NY, NZ)
    return apply_forcing(read, forcing), displacement
```

```python
import functools

import jax
import jax.numpy as jnp
from jax import lax
from jax.experimental import pallas as pl
from jax.experimental.pallas import tpu as pltpu
from jax.sharding import PartitionSpec as P

MESH = pl.DeviceIdType.MESH
F32 = jnp.float32
BF16 = jnp.bfloat16
LANES = 128

lattice_dirs = (
    (0, 0, 0),
    (1, 0, 0),
    (-1, 0, 0),
    (0, 1, 0),
    (0, -1, 0),
    (0, 0, 1),
    (0, 0, -1),
    (1, 1, 0),
    (-1, -1, 0),
    (1, -1, 0),
    (-1, 1, 0),
    (1, 0, 1),
    (-1, 0, -1),
    (1, 0, -1),
    (-1, 0, 1),
    (0, 1, 1),
    (0, -1, -1),
    (0, 1, -1),
    (0, -1, 1),
)
lattice_weights = (1.0 / 3.0,) + (1.0 / 18.0,) * 6 + (1.0 / 36.0,) * 12
relax_rate = 1.25
coupling = 0.1

x_up = [q for q in range(19) if lattice_dirs[q][0] == 1]
x_down = [q for q in range(19) if lattice_dirs[q][0] == -1]
y_up = [q for q in range(19) if lattice_dirs[q][1] == 1]
y_down = [q for q in range(19) if lattice_dirs[q][1] == -1]
diagonal = [q for q in range(19) if lattice_dirs[q][0] != 0 and lattice_dirs[q][1] != 0]


def combine_dirs(fields, direction):
    total = None
    for axis_pos in range(3):
        if direction[axis_pos] != 0:
            field = fields[axis_pos]
            if total is None:
                total = field if direction[axis_pos] == 1 else -field
            else:
                total = total + field if direction[axis_pos] == 1 else total - field
    return total


def halves(values):
    high = values.astype(BF16)
    low = (values - high.astype(F32)).astype(BF16)
    return high, low


def iota(shape, dim):
    return lax.broadcasted_iota(jnp.int32, shape, dim)


def dot_nt(left, right):
    return lax.dot_general(left, right, (((1,), (1,)), ((), ())), preferred_element_type=F32)


def dot_nn(left, right):
    return lax.dot_general(left, right, (((1,), (0,)), ((), ())), preferred_element_type=F32)


def collide_kernel(pop_ref, relaxed_ref, moment_ref, xu_ref, xd_ref, yu_ref, yd_ref):
    step = pl.program_id(0)
    last = pl.num_programs(0) - 1
    rows, cols, depth = pop_ref.shape[1:]

    def one(row, carry):
        pops = [pop_ref[q, row] for q in range(19)]
        density = pops[0]
        for q in range(1, 19):
            density = density + pops[q]
        moment = []
        for axis_pos in range(3):
            total = None
            for q in range(19):
                sign = lattice_dirs[q][axis_pos]
                if sign == 1:
                    total = pops[q] if total is None else total + pops[q]
                elif sign == -1:
                    total = -pops[q] if total is None else total - pops[q]
            moment.append(total)
            moment_ref[axis_pos, row] = total
        velocity = [moment[axis_pos] / density for axis_pos in range(3)]
        squared = (
            velocity[0] * velocity[0] + velocity[1] * velocity[1] + velocity[2] * velocity[2]
        )
        rest = 1.0 - 1.5 * squared
        for q in range(19):
            projected = combine_dirs(velocity, lattice_dirs[q])
            bracket = rest
            if projected is not None:
                bracket = rest + projected * (3.0 + 4.5 * projected)
            relaxed = (1.0 - relax_rate) * pops[q] + (
                relax_rate * lattice_weights[q]
            ) * density * bracket
            relaxed_ref[q, row] = relaxed
            if q in y_up:
                yu_ref[y_up.index(q), row] = relaxed[cols - 1 : cols]
            if q in y_down:
                yd_ref[y_down.index(q), row] = relaxed[0:1]
        return carry

    lax.fori_loop(0, rows, one, 0)

    @pl.when(step == 0)
    def _():
        for k, q in enumerate(x_down):
            xd_ref[k] = relaxed_ref[q, 0]

    @pl.when(step == last)
    def _():
        for k, q in enumerate(x_up):
            xu_ref[k] = relaxed_ref[q, rows - 1]


def collide(populations):
    _, nx, ny, nz = populations.shape
    rows = 8
    steps = nx // rows
    return pl.pallas_call(
        collide_kernel,
        grid=(steps,),
        in_specs=[pl.BlockSpec((19, rows, ny, nz), lambda i: (0, i, 0, 0))],
        out_specs=[
            pl.BlockSpec((19, rows, ny, nz), lambda i: (0, i, 0, 0)),
            pl.BlockSpec((3, rows, ny, nz), lambda i: (0, i, 0, 0)),
            pl.BlockSpec((5, ny, nz), lambda i: (0, 0, 0)),
            pl.BlockSpec((5, ny, nz), lambda i: (0, 0, 0)),
            pl.BlockSpec((5, rows, 1, nz), lambda i: (0, i, 0, 0)),
            pl.BlockSpec((5, rows, 1, nz), lambda i: (0, i, 0, 0)),
        ],
        out_shape=[
            jax.ShapeDtypeStruct((19, nx, ny, nz), F32),
            jax.ShapeDtypeStruct((3, nx, ny, nz), F32),
            jax.ShapeDtypeStruct((5, ny, nz), F32),
            jax.ShapeDtypeStruct((5, ny, nz), F32),
            jax.ShapeDtypeStruct((5, nx, 1, nz), F32),
            jax.ShapeDtypeStruct((5, nx, 1, nz), F32),
        ],
        compiler_params=pltpu.CompilerParams(dimension_semantics=("arbitrary",)),
        name="collide",
    )(populations)


def pack_kernel(
    devices, parts, node_cols, mom_ref, w_ref, blk_ref, own_ref, node_ref,
    out_ref, slot_ref, mom_cat, tri, base, acc,
):
    step = pl.program_id(0)
    blocks = mom_ref.shape[0] // 3
    chunk = w_ref.shape[0]

    @pl.when(step == 0)
    def _():
        high, low = halves(mom_ref[...])
        mom_cat[...] = jnp.concatenate([high, low, high], axis=1)
        before = iota((chunk, chunk), 0) <= iota((chunk, chunk), 1)
        tri[...] = before.astype(F32).astype(BF16)
        base[...] = jnp.zeros_like(base)
        acc[...] = jnp.zeros_like(acc)

    w_high, w_low = halves(w_ref[...])
    products = dot_nt(mom_cat[...], jnp.concatenate([w_high, w_high, w_low], axis=1))
    here = iota((blocks, chunk), 0) == blk_ref[...]
    loads = [
        jnp.sum(
            jnp.where(here, products[c * blocks : (c + 1) * blocks], 0.0), axis=0, keepdims=True
        )
        for c in range(3)
    ]
    owners = own_ref[...]
    hits = (iota((devices, chunk), 0) == owners).astype(F32)
    counts = dot_nn(hits.astype(BF16), tri[...])
    slots = jnp.sum(hits * (counts - 1.0 + base[:, 0:1]), axis=0, keepdims=True)
    base[...] = base[...] + counts[:, chunk - 1 : chunk]
    slot_id = slots.astype(jnp.int32)
    slot_ref[...] = slot_id
    part = slot_id // LANES
    place = slot_id - part * LANES
    node = node_ref[...]
    node_row = node // node_cols
    node_high = (node_row * node_cols).astype(F32)
    node_low = (node - node_row * node_cols).astype(F32)
    channel = iota((8, chunk), 0) // parts
    in_part = (iota((8, chunk), 0) - channel * parts) == part
    high_rows = jnp.zeros((8, chunk), F32)
    low_rows = jnp.zeros((8, chunk), F32)
    for c in range(4):
        if c < 3:
            high = loads[c].astype(BF16).astype(F32)
            low = loads[c] - high
        else:
            high, low = node_high, node_low
        high_rows = jnp.where(in_part & (channel == c), high, high_rows)
        low_rows = jnp.where(in_part & (channel == c), low, low_rows)
    mine = (iota((devices * 8, chunk), 0) // 8) == owners

    def spread(rows):
        tiled = jnp.broadcast_to(rows[None], (devices, 8, chunk)).reshape(devices * 8, chunk)
        return jnp.where(mine, tiled, 0.0).astype(BF16)

    slot_hot = (iota((LANES, chunk), 0) == place).astype(F32).astype(BF16)
    acc[...] += dot_nt(
        jnp.concatenate([spread(high_rows), spread(low_rows)], axis=1),
        jnp.concatenate([slot_hot, slot_hot], axis=1),
    )

    @pl.when(step == pl.num_programs(0) - 1)
    def _():
        out_ref[...] = acc[...].reshape(devices, 8, LANES)


def pack_loads(devices, parts, node_cols, moment, weights, blk, own, node):
    records, depth = weights.shape
    chunk = 512
    rows3 = moment.shape[0]
    row_spec = pl.BlockSpec((1, chunk), lambda i: (0, i))
    return pl.pallas_call(
        functools.partial(pack_kernel, devices, parts, node_cols),
        grid=(records // chunk,),
        in_specs=[
            pl.BlockSpec((rows3, depth), lambda i: (0, 0)),
            pl.BlockSpec((chunk, depth), lambda i: (i, 0)),
            row_spec,
            row_spec,
            row_spec,
        ],
        out_specs=[
            pl.BlockSpec((devices, 8, LANES), lambda i: (0, 0, 0)),
            row_spec,
        ],
        out_shape=[
            jax.ShapeDtypeStruct((devices, 8, LANES), F32),
            jax.ShapeDtypeStruct((1, records), jnp.int32),
        ],
        scratch_shapes=[
            pltpu.VMEM((rows3, 3 * depth), BF16),
            pltpu.VMEM((chunk, chunk), BF16),
            pltpu.VMEM((devices, LANES), F32),
            pltpu.VMEM((devices * 8, LANES), F32),
        ],
        compiler_params=pltpu.CompilerParams(dimension_semantics=("arbitrary",)),
        name="pack_loads",
    )(moment, weights, blk, own, node)


def position(grid):
    return lax.axis_index("gx"), lax.axis_index("gy")


def greet_all(grid):
    ix, iy = position(grid)
    devices = grid[0] * grid[1]
    me = ix * grid[1] + iy
    barrier = pltpu.get_barrier_semaphore()

    def signal(j, carry):
        other = lax.rem(me + j, devices)
        pl.semaphore_signal(
            barrier, inc=1, device_id=(other // grid[1], lax.rem(other, grid[1])),
            device_id_type=MESH,
        )
        return carry

    lax.fori_loop(1, devices, signal, 0)
    pl.semaphore_wait(barrier, devices - 1)


def broadcast_copy(grid, j, source, target, send_sem, recv_sem):
    ix, iy = position(grid)
    devices = grid[0] * grid[1]
    me = ix * grid[1] + iy
    other = lax.rem(me + j, devices)
    return pltpu.make_async_remote_copy(
        src_ref=source(other),
        dst_ref=target(me),
        send_sem=send_sem.at[j],
        recv_sem=recv_sem.at[j],
        device_id=(other // grid[1], lax.rem(other, grid[1])),
        device_id_type=MESH,
    )


def to_all(grid, source, target, send_sem, recv_sem, start):
    def body(j, carry):
        copy = broadcast_copy(grid, j, source, target, send_sem, recv_sem)
        if start:
            copy.start()
        else:
            copy.wait()
        return carry

    lax.fori_loop(1, grid[0] * grid[1], body, 0)


def neighbour_copy(grid, dx, dy, source, target, send_sem, recv_sem):
    ix, iy = position(grid)
    return pltpu.make_async_remote_copy(
        src_ref=source,
        dst_ref=target,
        send_sem=send_sem,
        recv_sem=recv_sem,
        device_id=(lax.rem(ix + dx + grid[0], grid[0]), lax.rem(iy + dy + grid[1], grid[1])),
        device_id_type=MESH,
    )


def rim_copies(grid, field, side, strip, send_sem, recv_sem):
    rows = field.shape[1]
    copies = [
        neighbour_copy(grid, 0, 1, field, side.at[0], send_sem.at[0], recv_sem.at[0]),
        neighbour_copy(grid, 0, -1, field, side.at[1], send_sem.at[1], recv_sem.at[1]),
    ]
    for k in range(3):
        dy = 1 - k
        copies.append(
            neighbour_copy(
                grid, 1, dy, field.at[:, pl.ds(rows - 8, 8), :], strip.at[k],
                send_sem.at[2 + k], recv_sem.at[2 + k],
            )
        )
    for k in range(3):
        dy = 1 - k
        copies.append(
            neighbour_copy(
                grid, -1, dy, field.at[:, pl.ds(0, 8), :], strip.at[3 + k],
                send_sem.at[5 + k], recv_sem.at[5 + k],
            )
        )
    return copies


def exchange_kernel(
    grid, pay, xu, xd, yu, yd, stat,
    pay_in, xu_in, xd_in, yu_in, yd_in, corner_in, side_in, strip_in,
    pay_send, pay_recv, lb_send, lb_recv, rim_send, rim_recv,
):
    ix, iy = position(grid)
    me = ix * grid[1] + iy
    greet_all(grid)
    to_all(grid, lambda o: pay.at[o], lambda m: pay_in.at[m], pay_send, pay_recv, True)
    nx = yu.shape[1]
    copies = rim_copies(grid, stat, side_in, strip_in, rim_send, rim_recv)
    plan = [
        (1, 0, xu, xu_in),
        (-1, 0, xd, xd_in),
        (0, 1, yu, yu_in),
        (0, -1, yd, yd_in),
    ]
    for k, q in enumerate(diagonal):
        dx, dy, _ = lattice_dirs[q]
        edge = yu.at[y_up.index(q)] if dy == 1 else yd.at[y_down.index(q)]
        plan.append((dx, dy, edge.at[nx - 1 if dx == 1 else 0], corner_in.at[k]))
    for number, (dx, dy, source, target) in enumerate(plan):
        copies.append(
            neighbour_copy(grid, dx, dy, source, target, lb_send.at[number], lb_recv.at[number])
        )
    for copy in copies:
        copy.start()
    pay_in[me] = pay[me]
    to_all(grid, lambda o: pay.at[o], lambda m: pay_in.at[m], pay_send, pay_recv, False)
    for copy in copies:
        copy.wait()


def exchange(grid, pay, xu, xd, yu, yd, stat):
    devices = grid[0] * grid[1]
    depth = xu.shape[2]
    shapes = [pay.shape, xu.shape, xd.shape, yu.shape, yd.shape, (4, 1, depth)]
    shapes += [(2,) + stat.shape, (6, stat.shape[0], 8, stat.shape[2])]
    vmem = pl.BlockSpec(memory_space=pltpu.VMEM)
    return pl.pallas_call(
        functools.partial(exchange_kernel, grid),
        in_specs=[vmem] * 6,
        out_specs=[vmem] * len(shapes),
        out_shape=[jax.ShapeDtypeStruct(shape, F32) for shape in shapes],
        scratch_shapes=[
            pltpu.SemaphoreType.DMA((devices,)),
            pltpu.SemaphoreType.DMA((devices,)),
            pltpu.SemaphoreType.DMA((8,)),
            pltpu.SemaphoreType.DMA((8,)),
            pltpu.SemaphoreType.DMA((8,)),
            pltpu.SemaphoreType.DMA((8,)),
        ],
        compiler_params=pltpu.CompilerParams(collective_id=0, has_side_effects=True),
        name="exchange",
    )(pay, xu, xd, yu, yd, stat)


def return_kernel(grid, pay, pay_in, pay_send, pay_recv):
    ix, iy = position(grid)
    me = ix * grid[1] + iy
    greet_all(grid)
    to_all(grid, lambda o: pay.at[o], lambda m: pay_in.at[m], pay_send, pay_recv, True)
    pay_in[me] = pay[me]
    to_all(grid, lambda o: pay.at[o], lambda m: pay_in.at[m], pay_send, pay_recv, False)


def send_back(grid, pay):
    devices = grid[0] * grid[1]
    vmem = pl.BlockSpec(memory_space=pltpu.VMEM)
    return pl.pallas_call(
        functools.partial(return_kernel, grid),
        in_specs=[vmem],
        out_specs=vmem,
        out_shape=jax.ShapeDtypeStruct(pay.shape, F32),
        scratch_shapes=[
            pltpu.SemaphoreType.DMA((devices,)),
            pltpu.SemaphoreType.DMA((devices,)),
        ],
        compiler_params=pltpu.CompilerParams(collective_id=2, has_side_effects=True),
        name="send_back",
    )(pay)


def joined(block, first, parts):
    return jnp.concatenate([block[first + p : first + p + 1] for p in range(parts)], axis=1)


def force_kernel(parts, pay_ref, force_ref):
    devices = pay_ref.shape[0]
    rows, cols = force_ref.shape[1:]
    width = parts * LANES

    def one(d, total):
        block = pay_ref[d]
        node = joined(block, 3 * parts, parts).astype(jnp.int32)
        row = node // cols
        col = node - row * cols
        row_hot = iota((rows, width), 0) == row
        col_hot = (iota((cols, width), 0) == col).astype(F32).astype(BF16)
        highs = []
        lows = []
        for c in range(3):
            value = joined(block, c * parts, parts)
            high = value.astype(BF16).astype(F32)
            highs.append(jnp.where(row_hot, high, 0.0))
            lows.append(jnp.where(row_hot, value - high, 0.0))
        left = jnp.concatenate(
            [jnp.concatenate(highs, axis=0).astype(BF16), jnp.concatenate(lows, axis=0).astype(BF16)],
            axis=1,
        )
        return total + dot_nt(left, jnp.concatenate([col_hot, col_hot], axis=1))

    total = lax.fori_loop(0, devices, one, jnp.zeros((3 * rows, cols), F32))
    for c in range(3):
        force_ref[c] = total[c * rows : (c + 1) * rows]


def force_of(parts, pay, rows, cols):
    return pl.pallas_call(
        functools.partial(force_kernel, parts),
        out_shape=jax.ShapeDtypeStruct((3, rows, cols), F32),
        name="force",
    )(pay)


def pick_kernel(parts, disp_ref, pay_ref, out_ref):
    devices = pay_ref.shape[0]
    rows, cols = disp_ref.shape[1:]
    width = parts * LANES
    high, low = halves(jnp.concatenate([disp_ref[c] for c in range(3)], axis=0))
    left = jnp.concatenate([high, low], axis=1)

    def one(d, carry):
        node = joined(pay_ref[d], 3 * parts, parts).astype(jnp.int32)
        row = node // cols
        col = node - row * cols
        row_hot = iota((rows, width), 0) == row
        col_hot = (iota((cols, width), 0) == col).astype(F32).astype(BF16)
        found = dot_nn(left, jnp.concatenate([col_hot, col_hot], axis=0))
        pieces = []
        for c in range(3):
            value = jnp.sum(
                jnp.where(row_hot, found[c * rows : (c + 1) * rows], 0.0), axis=0, keepdims=True
            )
            pieces += [value[:, p * LANES : (p + 1) * LANES] for p in range(parts)]
        pieces.append(jnp.zeros((8 - 3 * parts, LANES), F32))
        out_ref[d] = jnp.concatenate(pieces, axis=0)
        return carry

    lax.fori_loop(0, devices, one, 0)


def pick(parts, disp, pay):
    return pl.pallas_call(
        functools.partial(pick_kernel, parts),
        out_shape=jax.ShapeDtypeStruct(pay.shape, F32),
        name="pick",
    )(disp, pay)


def with_rim(centre, side, strip, c):
    rows, cols = centre.shape[1:]
    left_half = iota((rows, cols), 1) < cols // 2
    main = jnp.concatenate([centre[c], jnp.where(left_half, side[1, c], side[0, c])], axis=1)
    low = iota((8, cols), 0) < 4
    left_strip = iota((8, cols), 1) < cols // 2
    below = jnp.where(low, strip[4, c], strip[1, c])
    corner = jnp.where(
        low,
        jnp.where(left_strip, strip[5, c], strip[3, c]),
        jnp.where(left_strip, strip[2, c], strip[0, c]),
    )
    return jnp.concatenate([main, jnp.concatenate([below, corner], axis=1)], axis=0)


def solve_kernel(
    grid, stiff, force, stat, stat_side, stat_strip, disp,
    side, strip, one_buf, two_buf, rim_send, rim_recv, one_send, one_recv, two_send, two_recv,
):
    ix, iy = position(grid)
    me = ix * grid[1] + iy
    rows, cols = force.shape[1:]
    full = (rows + 8, 2 * cols)
    greet_all(grid)
    copies = rim_copies(grid, force, side, strip, rim_send, rim_recv)
    for copy in copies:
        copy.start()

    def back_row(a):
        return pltpu.roll(a, full[0] - 1, 0)

    def back_col(a):
        return pltpu.roll(a, full[1] - 1, 1)

    moduli = with_rim(stat, stat_side, stat_strip, 0)
    live = with_rim(stat, stat_side, stat_strip, 1)
    mass = with_rim(stat, stat_side, stat_strip, 2)
    next_row = back_row(moduli)
    scale = live * (moduli + next_row + back_col(moduli) + back_col(next_row)) * 0.25

    def operate(fields):
        down = [back_row(f) for f in fields]
        corners = (
            list(fields) + down + [back_col(f) for f in fields] + [back_col(f) for f in down]
        )
        results = []
        for k in range(12):
            total = stiff[k, 0] * corners[0]
            for l in range(1, 12):
                total = total + stiff[k, l] * corners[l]
            results.append(scale * total)
        images = []
        for c in range(3):
            right = results[6 + c] + pltpu.roll(results[9 + c], 1, 0)
            images.append(
                mass * fields[c]
                + results[c]
                + pltpu.roll(results[3 + c], 1, 0)
                + pltpu.roll(right, 1, 1)
            )
        return images

    def inner(a, b):
        total = a[0][:rows, :cols] * b[0][:rows, :cols]
        for c in range(1, 3):
            total = total + a[c][:rows, :cols] * b[c][:rows, :cols]
        return jnp.sum(jnp.sum(total, axis=0, keepdims=True), axis=1, keepdims=True)

    def sum_over_devices(values, buf, send_sem, recv_sem):
        lane = iota((1, LANES), 1)
        line = jnp.zeros((1, LANES), F32)
        for k, value in enumerate(values):
            line = jnp.where(lane == k, value, line)
        buf[me] = line
        source = lambda o: buf.at[me]
        target = lambda m: buf.at[m]
        to_all(grid, source, target, send_sem, recv_sem, True)
        to_all(grid, source, target, send_sem, recv_sem, False)
        total = jnp.sum(buf[...], axis=0)
        return [total[:, k : k + 1] for k in range(len(values))]

    for copy in copies:
        copy.wait()
    field = [with_rim(force, side, strip, c) for c in range(3)]
    image = operate(field)
    ff, fq = sum_over_devices(
        [inner(field, field), inner(field, image)], one_buf, one_send, one_recv
    )
    first = ff / fq
    residual = [field[c] - first * image[c] for c in range(3)]
    second_image = operate(residual)
    rr, rs, rq = sum_over_devices(
        [inner(residual, residual), inner(residual, second_image), inner(residual, image)],
        two_buf, two_send, two_recv,
    )
    ratio = rr / ff
    second = rr / (rs + 2.0 * ratio * rq + ratio * ratio * fq)
    for c in range(3):
        f = field[c][:rows, :cols]
        disp[c] = first * f + second * (residual[c][:rows, :cols] + ratio * f)


def solve(grid, stiff, force, stat, stat_side, stat_strip):
    devices = grid[0] * grid[1]
    vmem = pl.BlockSpec(memory_space=pltpu.VMEM)
    return pl.pallas_call(
        functools.partial(solve_kernel, grid),
        in_specs=[pl.BlockSpec(memory_space=pltpu.SMEM)] + [vmem] * 4,
        out_specs=vmem,
        out_shape=jax.ShapeDtypeStruct(force.shape, F32),
        scratch_shapes=[
            pltpu.VMEM((2,) + force.shape, F32),
            pltpu.VMEM((6, 3, 8, force.shape[2]), F32),
            pltpu.VMEM((devices, 1, LANES), F32),
            pltpu.VMEM((devices, 1, LANES), F32),
            pltpu.SemaphoreType.DMA((8,)),
            pltpu.SemaphoreType.DMA((8,)),
            pltpu.SemaphoreType.DMA((devices,)),
            pltpu.SemaphoreType.DMA((devices,)),
            pltpu.SemaphoreType.DMA((devices,)),
            pltpu.SemaphoreType.DMA((devices,)),
        ],
        compiler_params=pltpu.CompilerParams(collective_id=1, has_side_effects=True),
        name="solve",
    )(stiff, force, stat, stat_side, stat_strip)


def forcing_kernel(parts, back_ref, w_ref, blk_ref, own_ref, slot_ref, out_ref, back_cat):
    step = pl.program_id(0)
    devices = back_ref.shape[0]
    blocks = out_ref.shape[0] // 3
    chunk = w_ref.shape[0]

    @pl.when(step == 0)
    def _():
        high, low = halves(back_ref[...].reshape(devices * 8, LANES))
        back_cat[...] = jnp.concatenate([high, low], axis=1)
        out_ref[...] = jnp.zeros_like(out_ref)

    slot_id = slot_ref[...]
    part = slot_id // LANES
    place = slot_id - part * LANES
    slot_hot = (iota((LANES, chunk), 0) == place).astype(F32).astype(BF16)
    found = dot_nn(back_cat[...], jnp.concatenate([slot_hot, slot_hot], axis=0))
    mine = (iota((devices * 8, chunk), 0) // 8) == own_ref[...]
    lines = jnp.sum(jnp.where(mine, found, 0.0).reshape(devices, 8, chunk), axis=0)
    channel = iota((8, chunk), 0) // parts
    in_part = (iota((8, chunk), 0) - channel * parts) == part
    here = iota((blocks, chunk), 0) == blk_ref[...]
    highs = []
    lows = []
    for c in range(3):
        moved = coupling * jnp.sum(
            jnp.where(in_part & (channel == c), lines, 0.0), axis=0, keepdims=True
        )
        high = moved.astype(BF16).astype(F32)
        highs.append(jnp.where(here, high, 0.0).astype(BF16))
        lows.append(jnp.where(here, moved - high, 0.0).astype(BF16))
    high = jnp.concatenate(highs, axis=0)
    low = jnp.concatenate(lows, axis=0)
    w_high, w_low = halves(w_ref[...])
    out_ref[...] += dot_nn(
        jnp.concatenate([high, low, high], axis=1),
        jnp.concatenate([w_high, w_high, w_low], axis=0),
    )


def forcing_of(parts, blocks, back, weights, blk, own, slot):
    records, depth = weights.shape
    chunk = 512
    row_spec = pl.BlockSpec((1, chunk), lambda i: (0, i))
    return pl.pallas_call(
        functools.partial(forcing_kernel, parts),
        grid=(records // chunk,),
        in_specs=[
            pl.BlockSpec(back.shape, lambda i: (0, 0, 0)),
            pl.BlockSpec((chunk, depth), lambda i: (i, 0)),
            row_spec,
            row_spec,
            row_spec,
        ],
        out_specs=pl.BlockSpec((3 * blocks, depth), lambda i: (0, 0)),
        out_shape=jax.ShapeDtypeStruct((3 * blocks, depth), F32),
        scratch_shapes=[pltpu.VMEM((back.shape[0] * 8, 2 * LANES), BF16)],
        compiler_params=pltpu.CompilerParams(dimension_semantics=("arbitrary",)),
        name="forcing",
    )(back, weights, blk, own, slot)


def stream_kernel(
    cur, prev_ref, next_ref, forcing, xu, xd, yu, yd, yu_prev, yu_next, yd_prev, yd_next, corner,
    out_ref,
):
    step = pl.program_id(0)
    last = pl.num_programs(0) - 1
    rows, ny, nz = cur.shape[1:]
    fields = [forcing[c] for c in range(3)]

    def shifted(block, before, after, dx):
        if dx == 1:
            return jnp.concatenate([before[None], block[: rows - 1]], axis=0)
        if dx == -1:
            return jnp.concatenate([block[1:], after[None]], axis=0)
        return block

    for q in range(19):
        dx, dy, dz = lattice_dirs[q]
        before = after = None
        if dx == 1:
            before = jnp.where(step == 0, xu[x_up.index(q)], prev_ref[q, 0])
        if dx == -1:
            after = jnp.where(step == last, xd[x_down.index(q)], next_ref[q, 0])
        moved = shifted(cur[q], before, after, dx)
        if dy != 0:
            k = y_up.index(q) if dy == 1 else y_down.index(q)
            edge = (yu if dy == 1 else yd)[k]
            if dx == 1:
                before = (yu_prev if dy == 1 else yd_prev)[k, 0]
                before = jnp.where(step == 0, corner[diagonal.index(q)], before)
            if dx == -1:
                after = (yu_next if dy == 1 else yd_next)[k, 0]
                after = jnp.where(step == last, corner[diagonal.index(q)], after)
            edge = shifted(edge, before, after, dx)
            turned = pltpu.roll(moved, dy % ny, 1)
            at_edge = iota((rows, ny, nz), 1) == (0 if dy == 1 else ny - 1)
            moved = jnp.where(at_edge, jnp.broadcast_to(edge, (rows, ny, nz)), turned)
        if dz != 0:
            moved = pltpu.roll(moved, dz % nz, 2)
        projected = combine_dirs(fields, lattice_dirs[q])
        if projected is not None:
            moved = moved + (3.0 * lattice_weights[q]) * projected
        out_ref[q] = moved


def stream(relaxed, forcing, xu, xd, yu, yd, corner):
    _, nx, ny, nz = relaxed.shape
    rows = 4
    steps = nx // rows
    before = lambda i: (0, (i * rows + nx - 1) % nx, 0, 0)
    after = lambda i: (0, (i * rows + rows) % nx, 0, 0)
    whole3 = lambda i: (0, 0, 0)
    blocked = lambda i: (0, i, 0, 0)
    return pl.pallas_call(
        stream_kernel,
        grid=(steps,),
        in_specs=[
            pl.BlockSpec((19, rows, ny, nz), blocked),
            pl.BlockSpec((19, 1, ny, nz), before),
            pl.BlockSpec((19, 1, ny, nz), after),
            pl.BlockSpec((3, rows, ny, nz), blocked),
            pl.BlockSpec((5, ny, nz), whole3),
            pl.BlockSpec((5, ny, nz), whole3),
            pl.BlockSpec((5, rows, 1, nz), blocked),
            pl.BlockSpec((5, rows, 1, nz), blocked),
            pl.BlockSpec((5, 1, 1, nz), before),
            pl.BlockSpec((5, 1, 1, nz), after),
            pl.BlockSpec((5, 1, 1, nz), before),
            pl.BlockSpec((5, 1, 1, nz), after),
            pl.BlockSpec((4, 1, nz), whole3),
        ],
        out_specs=pl.BlockSpec((19, rows, ny, nz), blocked),
        out_shape=jax.ShapeDtypeStruct((19, nx, ny, nz), F32),
        compiler_params=pltpu.CompilerParams(dimension_semantics=("arbitrary",)),
        name="stream",
    )(relaxed, relaxed, relaxed, forcing, xu, xd, yu, yd, yu, yu, yd, yd, corner)


def per_device(
    grid, populations, mass, modulus, cell_live, stiff_ref, rec_block, rec_owner, rec_node,
    rbf_weight,
):
    devices = grid[0] * grid[1]
    _, nx, ny, nz = populations.shape
    records = rec_block.shape[0]
    rows, cols = mass.shape
    capacity = 2 * records // devices
    parts = -(-capacity // LANES)
    relaxed, moment, xu, xd, yu, yd = collide(populations)
    blk = rec_block.reshape(1, records)
    own = rec_owner.reshape(1, records)
    node = rec_node.reshape(1, records)
    stat = jnp.stack([modulus, cell_live.astype(F32), mass])
    pay, slot = pack_loads(
        devices, parts, cols, moment.reshape(3 * nx * ny, nz), rbf_weight, blk, own, node
    )
    pay, xu, xd, yu, yd, corner, side, strip = exchange(grid, pay, xu, xd, yu, yd, stat)
    force = force_of(parts, pay, rows, cols)
    displacement = solve(grid, stiff_ref, force, stat, side, strip)
    back = send_back(grid, pick(parts, displacement, pay))
    forcing = forcing_of(parts, nx * ny, back, rbf_weight, blk, own, slot)
    out = stream(relaxed, forcing.reshape(3, nx, ny, nz), xu, xd, yu, yd, corner)
    return out, displacement


def solution(mesh):
    grid = (mesh.shape["gx"], mesh.shape["gy"])
    in_specs = (
        P(None, "gx", "gy", None),
        P("gx", "gy"),
        P("gx", "gy"),
        P("gx", "gy"),
        P(),
        P(("gx", "gy")),
        P(("gx", "gy"), None),
        P(("gx", "gy")),
        P(("gx", "gy"), None),
    )
    out_specs = (P(None, "gx", "gy", None), P(None, "gx", "gy"))
    return jax.shard_map(
        functools.partial(per_device, grid), mesh=mesh, in_specs=in_specs, out_specs=out_specs,
        check_vma=False,
    )
```

```python
import functools
import math

import jax
import jax.numpy as jnp
from jax import lax
from jax.experimental import pallas as pl
from jax.experimental.pallas import tpu as pltpu
from jax.sharding import PartitionSpec as P

MESH = pl.DeviceIdType.MESH
F32 = jnp.float32
BF16 = jnp.bfloat16
LANES = 128

lattice_dirs = (
    (0, 0, 0),
    (1, 0, 0),
    (-1, 0, 0),
    (0, 1, 0),
    (0, -1, 0),
    (0, 0, 1),
    (0, 0, -1),
    (1, 1, 0),
    (-1, -1, 0),
    (1, -1, 0),
    (-1, 1, 0),
    (1, 0, 1),
    (-1, 0, -1),
    (1, 0, -1),
    (-1, 0, 1),
    (0, 1, 1),
    (0, -1, -1),
    (0, 1, -1),
    (0, -1, 1),
)
lattice_weights = (1.0 / 3.0,) + (1.0 / 18.0,) * 6 + (1.0 / 36.0,) * 12
relax_rate = 1.25
coupling = 0.1

x_up = [q for q in range(19) if lattice_dirs[q][0] == 1]
x_down = [q for q in range(19) if lattice_dirs[q][0] == -1]
y_up = [q for q in range(19) if lattice_dirs[q][1] == 1]
y_down = [q for q in range(19) if lattice_dirs[q][1] == -1]
diagonal = [q for q in range(19) if lattice_dirs[q][0] != 0 and lattice_dirs[q][1] != 0]


def combine_dirs(fields, direction):
    total = None
    for axis_pos in range(3):
        if direction[axis_pos] != 0:
            field = fields[axis_pos]
            if total is None:
                total = field if direction[axis_pos] == 1 else -field
            else:
                total = total + field if direction[axis_pos] == 1 else total - field
    return total


def halves(values):
    high = values.astype(BF16)
    low = (values - high.astype(F32)).astype(BF16)
    return high, low


def iota(shape, dim):
    return lax.broadcasted_iota(jnp.int32, shape, dim)


def dot_nt(left, right):
    return lax.dot_general(left, right, (((1,), (1,)), ((), ())), preferred_element_type=F32)


def dot_nn(left, right):
    return lax.dot_general(left, right, (((1,), (0,)), ((), ())), preferred_element_type=F32)


def collide_kernel(pop_ref, relaxed_ref, moment_ref, xu_ref, xd_ref, yu_ref, yd_ref):
    step = pl.program_id(0)
    last = pl.num_programs(0) - 1
    rows, cols, depth = pop_ref.shape[1:]

    def one(row, carry):
        pops = [pop_ref[q, row] for q in range(19)]
        density = pops[0]
        for q in range(1, 19):
            density = density + pops[q]
        moment = []
        for axis_pos in range(3):
            total = None
            for q in range(19):
                sign = lattice_dirs[q][axis_pos]
                if sign == 1:
                    total = pops[q] if total is None else total + pops[q]
                elif sign == -1:
                    total = -pops[q] if total is None else total - pops[q]
            moment.append(total)
            moment_ref[axis_pos, row] = total
        velocity = [moment[axis_pos] / density for axis_pos in range(3)]
        squared = (
            velocity[0] * velocity[0] + velocity[1] * velocity[1] + velocity[2] * velocity[2]
        )
        rest = 1.0 - 1.5 * squared
        for q in range(19):
            projected = combine_dirs(velocity, lattice_dirs[q])
            bracket = rest
            if projected is not None:
                bracket = rest + projected * (3.0 + 4.5 * projected)
            relaxed = (1.0 - relax_rate) * pops[q] + (
                relax_rate * lattice_weights[q]
            ) * density * bracket
            relaxed_ref[q, row] = relaxed
            if q in y_up:
                yu_ref[y_up.index(q), row] = relaxed[cols - 1 : cols]
            if q in y_down:
                yd_ref[y_down.index(q), row] = relaxed[0:1]
        return carry

    lax.fori_loop(0, rows, one, 0)

    @pl.when(step == 0)
    def _():
        for k, q in enumerate(x_down):
            xd_ref[k] = relaxed_ref[q, 0]

    @pl.when(step == last)
    def _():
        for k, q in enumerate(x_up):
            xu_ref[k] = relaxed_ref[q, rows - 1]


def collide(populations):
    _, nx, ny, nz = populations.shape
    rows = 8
    steps = nx // rows
    return pl.pallas_call(
        collide_kernel,
        grid=(steps,),
        in_specs=[pl.BlockSpec((19, rows, ny, nz), lambda i: (0, i, 0, 0))],
        out_specs=[
            pl.BlockSpec((19, rows, ny, nz), lambda i: (0, i, 0, 0)),
            pl.BlockSpec((3, rows, ny, nz), lambda i: (0, i, 0, 0)),
            pl.BlockSpec((5, ny, nz), lambda i: (0, 0, 0)),
            pl.BlockSpec((5, ny, nz), lambda i: (0, 0, 0)),
            pl.BlockSpec((5, rows, 1, nz), lambda i: (0, i, 0, 0)),
            pl.BlockSpec((5, rows, 1, nz), lambda i: (0, i, 0, 0)),
        ],
        out_shape=[
            jax.ShapeDtypeStruct((19, nx, ny, nz), F32),
            jax.ShapeDtypeStruct((3, nx, ny, nz), F32),
            jax.ShapeDtypeStruct((5, ny, nz), F32),
            jax.ShapeDtypeStruct((5, ny, nz), F32),
            jax.ShapeDtypeStruct((5, nx, 1, nz), F32),
            jax.ShapeDtypeStruct((5, nx, 1, nz), F32),
        ],
        compiler_params=pltpu.CompilerParams(dimension_semantics=("arbitrary",)),
        name="collide",
    )(populations)


def pack_kernel(
    devices, parts, node_cols, mom_ref, w_ref, blk_ref, own_ref, node_ref,
    out_ref, slot_ref, mom_cat, tri, base, acc,
):
    step = pl.program_id(0)
    blocks = mom_ref.shape[0] // 3
    chunk = w_ref.shape[0]

    @pl.when(step == 0)
    def _():
        high, low = halves(mom_ref[...])
        mom_cat[...] = jnp.concatenate([high, low, high], axis=1)
        before = iota((chunk, chunk), 0) <= iota((chunk, chunk), 1)
        tri[...] = before.astype(F32).astype(BF16)
        base[...] = jnp.zeros_like(base)
        acc[...] = jnp.zeros_like(acc)

    w_high, w_low = halves(w_ref[...])
    products = dot_nt(mom_cat[...], jnp.concatenate([w_high, w_high, w_low], axis=1))
    here = iota((blocks, chunk), 0) == blk_ref[...]
    loads = [
        jnp.sum(
            jnp.where(here, products[c * blocks : (c + 1) * blocks], 0.0), axis=0, keepdims=True
        )
        for c in range(3)
    ]
    owners = own_ref[...]
    hits = (iota((devices, chunk), 0) == owners).astype(F32)
    counts = dot_nn(hits.astype(BF16), tri[...])
    slots = jnp.sum(hits * (counts - 1.0 + base[:, 0:1]), axis=0, keepdims=True)
    base[...] = base[...] + counts[:, chunk - 1 : chunk]
    slot_id = slots.astype(jnp.int32)
    slot_ref[...] = slot_id
    part = slot_id // LANES
    place = slot_id - part * LANES
    node = node_ref[...]
    node_row = node // node_cols
    node_high = (node_row * node_cols).astype(F32)
    node_low = (node - node_row * node_cols).astype(F32)
    channel = iota((8, chunk), 0) // parts
    in_part = (iota((8, chunk), 0) - channel * parts) == part
    high_rows = jnp.zeros((8, chunk), F32)
    low_rows = jnp.zeros((8, chunk), F32)
    for c in range(4):
        if c < 3:
            high = loads[c].astype(BF16).astype(F32)
            low = loads[c] - high
        else:
            high, low = node_high, node_low
        high_rows = jnp.where(in_part & (channel == c), high, high_rows)
        low_rows = jnp.where(in_part & (channel == c), low, low_rows)
    mine = (iota((devices * 8, chunk), 0) // 8) == owners

    def spread(rows):
        tiled = jnp.broadcast_to(rows[None], (devices, 8, chunk)).reshape(devices * 8, chunk)
        return jnp.where(mine, tiled, 0.0).astype(BF16)

    slot_hot = (iota((LANES, chunk), 0) == place).astype(F32).astype(BF16)
    acc[...] += dot_nt(
        jnp.concatenate([spread(high_rows), spread(low_rows)], axis=1),
        jnp.concatenate([slot_hot, slot_hot], axis=1),
    )

    @pl.when(step == pl.num_programs(0) - 1)
    def _():
        out_ref[...] = acc[...].reshape(devices, 8, LANES)


def pack_loads(devices, parts, node_cols, moment, weights, blk, own, node):
    records, depth = weights.shape
    chunk = 512
    rows3 = moment.shape[0]
    row_spec = pl.BlockSpec((1, chunk), lambda i: (0, i))
    return pl.pallas_call(
        functools.partial(pack_kernel, devices, parts, node_cols),
        grid=(records // chunk,),
        in_specs=[
            pl.BlockSpec((rows3, depth), lambda i: (0, 0)),
            pl.BlockSpec((chunk, depth), lambda i: (i, 0)),
            row_spec,
            row_spec,
            row_spec,
        ],
        out_specs=[
            pl.BlockSpec((devices, 8, LANES), lambda i: (0, 0, 0)),
            row_spec,
        ],
        out_shape=[
            jax.ShapeDtypeStruct((devices, 8, LANES), F32),
            jax.ShapeDtypeStruct((1, records), jnp.int32),
        ],
        scratch_shapes=[
            pltpu.VMEM((rows3, 3 * depth), BF16),
            pltpu.VMEM((chunk, chunk), BF16),
            pltpu.VMEM((devices, LANES), F32),
            pltpu.VMEM((devices * 8, LANES), F32),
        ],
        compiler_params=pltpu.CompilerParams(dimension_semantics=("arbitrary",)),
        name="pack_loads",
    )(moment, weights, blk, own, node)


def position(grid):
    return lax.axis_index("gx"), lax.axis_index("gy")


def greet_all(grid):
    ix, iy = position(grid)
    devices = grid[0] * grid[1]
    me = ix * grid[1] + iy
    barrier = pltpu.get_barrier_semaphore()

    def signal(j, carry):
        other = lax.rem(me + j, devices)
        pl.semaphore_signal(
            barrier, inc=1, device_id=(other // grid[1], lax.rem(other, grid[1])),
            device_id_type=MESH,
        )
        return carry

    lax.fori_loop(1, devices, signal, 0)
    pl.semaphore_wait(barrier, devices - 1)


def broadcast_copy(grid, j, source, target, send_sem, recv_sem):
    ix, iy = position(grid)
    devices = grid[0] * grid[1]
    me = ix * grid[1] + iy
    other = lax.rem(me + j, devices)
    return pltpu.make_async_remote_copy(
        src_ref=source(other),
        dst_ref=target(me),
        send_sem=send_sem.at[j],
        recv_sem=recv_sem.at[j],
        device_id=(other // grid[1], lax.rem(other, grid[1])),
        device_id_type=MESH,
    )


def to_all(grid, source, target, send_sem, recv_sem, start):
    def body(j, carry):
        copy = broadcast_copy(grid, j, source, target, send_sem, recv_sem)
        if start:
            copy.start()
        else:
            copy.wait()
        return carry

    lax.fori_loop(1, grid[0] * grid[1], body, 0)


def neighbour_copy(grid, dx, dy, source, target, send_sem, recv_sem):
    ix, iy = position(grid)
    return pltpu.make_async_remote_copy(
        src_ref=source,
        dst_ref=target,
        send_sem=send_sem,
        recv_sem=recv_sem,
        device_id=(lax.rem(ix + dx + grid[0], grid[0]), lax.rem(iy + dy + grid[1], grid[1])),
        device_id_type=MESH,
    )


def rim_copies(grid, field, side, strip, send_sem, recv_sem):
    rows = field.shape[1]
    copies = [
        neighbour_copy(grid, 0, 1, field, side.at[0], send_sem.at[0], recv_sem.at[0]),
        neighbour_copy(grid, 0, -1, field, side.at[1], send_sem.at[1], recv_sem.at[1]),
    ]
    for k in range(3):
        dy = 1 - k
        copies.append(
            neighbour_copy(
                grid, 1, dy, field.at[:, pl.ds(rows - 8, 8), :], strip.at[k],
                send_sem.at[2 + k], recv_sem.at[2 + k],
            )
        )
    for k in range(3):
        dy = 1 - k
        copies.append(
            neighbour_copy(
                grid, -1, dy, field.at[:, pl.ds(0, 8), :], strip.at[3 + k],
                send_sem.at[5 + k], recv_sem.at[5 + k],
            )
        )
    return copies


def lines_of(ref, first, count, row, parts):
    return jnp.concatenate(
        [ref[first + d, row + p : row + p + 1] for d in range(count) for p in range(parts)],
        axis=1,
    )


def node_hots(ref, first, count, parts, rows, cols):
    node = lines_of(ref, first, count, 3 * parts, parts).astype(jnp.int32)
    row = node // cols
    col = node - row * cols
    width = count * parts * LANES
    row_hot = iota((rows, width), 0) == row
    col_hot = (iota((cols, width), 0) == col).astype(F32).astype(BF16)
    return row_hot, col_hot


def gather_force(parts, pay, force):
    devices = pay.shape[0]
    rows, cols = force.shape[1:]
    count = math.gcd(devices, 4)

    def one(step, total):
        first = step * count
        row_hot, col_hot = node_hots(pay, first, count, parts, rows, cols)
        highs = []
        lows = []
        for c in range(3):
            value = lines_of(pay, first, count, c * parts, parts)
            high = value.astype(BF16).astype(F32)
            highs.append(jnp.where(row_hot, high, 0.0).astype(BF16))
            lows.append(jnp.where(row_hot, value - high, 0.0).astype(BF16))
        left = jnp.concatenate(
            [jnp.concatenate(highs, axis=0), jnp.concatenate(lows, axis=0)], axis=1
        )
        return total + dot_nt(left, jnp.concatenate([col_hot, col_hot], axis=1))

    total = lax.fori_loop(0, devices // count, one, jnp.zeros((3 * rows, cols), F32))
    for c in range(3):
        force[c] = total[c * rows : (c + 1) * rows]


def pick_moved(parts, disp, pay, out):
    devices = pay.shape[0]
    rows, cols = disp[0].shape
    count = math.gcd(devices, 4)
    high, low = halves(jnp.concatenate(disp, axis=0))
    left = jnp.concatenate([high, low], axis=1)

    def one(step, carry):
        first = step * count
        row_hot, col_hot = node_hots(pay, first, count, parts, rows, cols)
        found = dot_nn(left, jnp.concatenate([col_hot, col_hot], axis=0))
        values = [
            jnp.sum(
                jnp.where(row_hot, found[c * rows : (c + 1) * rows], 0.0), axis=0, keepdims=True
            )
            for c in range(3)
        ]
        for d in range(count):
            pieces = []
            for value in values:
                for p in range(parts):
                    at = (d * parts + p) * LANES
                    pieces.append(value[:, at : at + LANES])
            pieces.append(jnp.zeros((8 - 3 * parts, LANES), F32))
            out[first + d] = jnp.concatenate(pieces, axis=0)
        return carry

    lax.fori_loop(0, devices // count, one, 0)


def with_rim(centre, side, strip, c):
    rows, cols = centre.shape[1:]
    left_half = iota((rows, cols), 1) < cols // 2
    main = jnp.concatenate([centre[c], jnp.where(left_half, side[1, c], side[0, c])], axis=1)
    low = iota((8, cols), 0) < 4
    left_strip = iota((8, cols), 1) < cols // 2
    below = jnp.where(low, strip[4, c], strip[1, c])
    corner = jnp.where(
        low,
        jnp.where(left_strip, strip[5, c], strip[3, c]),
        jnp.where(left_strip, strip[2, c], strip[0, c]),
    )
    return jnp.concatenate([main, jnp.concatenate([below, corner], axis=1)], axis=0)


def couple_kernel(
    grid, parts, stiff, pay, xu, xd, yu, yd, modulus_ref, live_ref, mass_ref,
    disp, back_in, xu_in, xd_in, yu_in, yd_in, corner_in,
    pay_in, back, stat, stat_side, stat_strip, force, side, strip, one_buf, two_buf,
    pay_send, pay_recv, back_send, back_recv, lb_send, lb_recv,
    stat_send, stat_recv, rim_send, rim_recv, one_send, one_recv, two_send, two_recv,
):
    ix, iy = position(grid)
    me = ix * grid[1] + iy
    rows, cols = force.shape[1:]
    full = (rows + 8, 2 * cols)
    stat[0] = modulus_ref[...]
    stat[1] = live_ref[...].astype(F32)
    stat[2] = mass_ref[...]
    greet_all(grid)
    to_all(grid, lambda o: pay.at[o], lambda m: pay_in.at[m], pay_send, pay_recv, True)
    stat_copies = rim_copies(grid, stat, stat_side, stat_strip, stat_send, stat_recv)
    nx = yu.shape[1]
    plan = [
        (1, 0, xu, xu_in),
        (-1, 0, xd, xd_in),
        (0, 1, yu, yu_in),
        (0, -1, yd, yd_in),
    ]
    for k, q in enumerate(diagonal):
        dx, dy, _ = lattice_dirs[q]
        edge = yu.at[y_up.index(q)] if dy == 1 else yd.at[y_down.index(q)]
        plan.append((dx, dy, edge.at[nx - 1 if dx == 1 else 0], corner_in.at[k]))
    lb_copies = [
        neighbour_copy(grid, dx, dy, source, target, lb_send.at[number], lb_recv.at[number])
        for number, (dx, dy, source, target) in enumerate(plan)
    ]
    pay_in[me] = pay[me]
    to_all(grid, lambda o: pay.at[o], lambda m: pay_in.at[m], pay_send, pay_recv, False)
    for copy in stat_copies + lb_copies:
        copy.start()
    gather_force(parts, pay_in, force)
    copies = rim_copies(grid, force, side, strip, rim_send, rim_recv)
    for copy in copies:
        copy.start()

    def back_row(a):
        return pltpu.roll(a, full[0] - 1, 0)

    def back_col(a):
        return pltpu.roll(a, full[1] - 1, 1)

    for copy in stat_copies:
        copy.wait()
    moduli = with_rim(stat, stat_side, stat_strip, 0)
    live = with_rim(stat, stat_side, stat_strip, 1)
    mass = with_rim(stat, stat_side, stat_strip, 2)
    next_row = back_row(moduli)
    scale = live * (moduli + next_row + back_col(moduli) + back_col(next_row)) * 0.25

    def operate(fields):
        down = [back_row(f) for f in fields]
        corners = (
            list(fields) + down + [back_col(f) for f in fields] + [back_col(f) for f in down]
        )
        results = []
        for k in range(12):
            total = stiff[k, 0] * corners[0]
            for l in range(1, 12):
                total = total + stiff[k, l] * corners[l]
            results.append(scale * total)
        images = []
        for c in range(3):
            right = results[6 + c] + pltpu.roll(results[9 + c], 1, 0)
            images.append(
                mass * fields[c]
                + results[c]
                + pltpu.roll(results[3 + c], 1, 0)
                + pltpu.roll(right, 1, 1)
            )
        return images

    def inner(a, b):
        total = a[0][:rows, :cols] * b[0][:rows, :cols]
        for c in range(1, 3):
            total = total + a[c][:rows, :cols] * b[c][:rows, :cols]
        return jnp.sum(jnp.sum(total, axis=0, keepdims=True), axis=1, keepdims=True)

    def sum_over_devices(values, buf, send_sem, recv_sem):
        lane = iota((1, LANES), 1)
        line = jnp.zeros((1, LANES), F32)
        for k, value in enumerate(values):
            line = jnp.where(lane == k, value, line)
        buf[me] = line
        source = lambda o: buf.at[me]
        target = lambda m: buf.at[m]
        to_all(grid, source, target, send_sem, recv_sem, True)
        to_all(grid, source, target, send_sem, recv_sem, False)
        total = jnp.sum(buf[...], axis=0)
        return [total[:, k : k + 1] for k in range(len(values))]

    for copy in copies:
        copy.wait()
    field = [with_rim(force, side, strip, c) for c in range(3)]
    image = operate(field)
    ff, fq = sum_over_devices(
        [inner(field, field), inner(field, image)], one_buf, one_send, one_recv
    )
    first = ff / fq
    residual = [field[c] - first * image[c] for c in range(3)]
    second_image = operate(residual)
    rr, rs, rq = sum_over_devices(
        [inner(residual, residual), inner(residual, second_image), inner(residual, image)],
        two_buf, two_send, two_recv,
    )
    ratio = rr / ff
    second = rr / (rs + 2.0 * ratio * rq + ratio * ratio * fq)
    moved = []
    for c in range(3):
        f = field[c][:rows, :cols]
        moved.append(first * f + second * (residual[c][:rows, :cols] + ratio * f))
        disp[c] = moved[c]
    pick_moved(parts, moved, pay_in, back)
    to_all(grid, lambda o: back.at[o], lambda m: back_in.at[m], back_send, back_recv, True)
    back_in[me] = back[me]
    to_all(grid, lambda o: back.at[o], lambda m: back_in.at[m], back_send, back_recv, False)
    for copy in lb_copies:
        copy.wait()


def couple(grid, parts, stiff, pay, xu, xd, yu, yd, modulus, live, mass):
    devices = grid[0] * grid[1]
    depth = xu.shape[2]
    patch = (3,) + mass.shape
    shapes = [patch, pay.shape, xu.shape, xd.shape, yu.shape, yd.shape, (4, 1, depth)]
    vmem = pl.BlockSpec(memory_space=pltpu.VMEM)
    rim = [pltpu.VMEM((2,) + patch, F32), pltpu.VMEM((6, 3, 8, patch[2]), F32)]
    to_each = pltpu.SemaphoreType.DMA((devices,))
    to_near = pltpu.SemaphoreType.DMA((8,))
    return pl.pallas_call(
        functools.partial(couple_kernel, grid, parts),
        in_specs=[pl.BlockSpec(memory_space=pltpu.SMEM)] + [vmem] * 8,
        out_specs=[vmem] * len(shapes),
        out_shape=[jax.ShapeDtypeStruct(shape, F32) for shape in shapes],
        scratch_shapes=[
            pltpu.VMEM(pay.shape, F32),
            pltpu.VMEM(pay.shape, F32),
            pltpu.VMEM(patch, F32),
            *rim,
            pltpu.VMEM(patch, F32),
            *rim,
            pltpu.VMEM((devices, 1, LANES), F32),
            pltpu.VMEM((devices, 1, LANES), F32),
            to_each, to_each, to_each, to_each, to_near, to_near,
            to_near, to_near, to_near, to_near, to_each, to_each, to_each, to_each,
        ],
        compiler_params=pltpu.CompilerParams(collective_id=0, has_side_effects=True),
        name="couple",
    )(stiff, pay, xu, xd, yu, yd, modulus, live, mass)


def forcing_kernel(parts, back_ref, w_ref, blk_ref, own_ref, slot_ref, out_ref, back_cat):
    step = pl.program_id(0)
    devices = back_ref.shape[0]
    blocks = out_ref.shape[0] // 3
    chunk = w_ref.shape[0]

    @pl.when(step == 0)
    def _():
        high, low = halves(back_ref[...].reshape(devices * 8, LANES))
        back_cat[...] = jnp.concatenate([high, low], axis=1)
        out_ref[...] = jnp.zeros_like(out_ref)

    slot_id = slot_ref[...]
    part = slot_id // LANES
    place = slot_id - part * LANES
    slot_hot = (iota((LANES, chunk), 0) == place).astype(F32).astype(BF16)
    found = dot_nn(back_cat[...], jnp.concatenate([slot_hot, slot_hot], axis=0))
    mine = (iota((devices * 8, chunk), 0) // 8) == own_ref[...]
    lines = jnp.sum(jnp.where(mine, found, 0.0).reshape(devices, 8, chunk), axis=0)
    channel = iota((8, chunk), 0) // parts
    in_part = (iota((8, chunk), 0) - channel * parts) == part
    here = iota((blocks, chunk), 0) == blk_ref[...]
    highs = []
    lows = []
    for c in range(3):
        moved = coupling * jnp.sum(
            jnp.where(in_part & (channel == c), lines, 0.0), axis=0, keepdims=True
        )
        high = moved.astype(BF16).astype(F32)
        highs.append(jnp.where(here, high, 0.0).astype(BF16))
        lows.append(jnp.where(here, moved - high, 0.0).astype(BF16))
    high = jnp.concatenate(highs, axis=0)
    low = jnp.concatenate(lows, axis=0)
    w_high, w_low = halves(w_ref[...])
    out_ref[...] += dot_nn(
        jnp.concatenate([high, low, high], axis=1),
        jnp.concatenate([w_high, w_high, w_low], axis=0),
    )


def forcing_of(parts, blocks, back, weights, blk, own, slot):
    records, depth = weights.shape
    chunk = 512
    row_spec = pl.BlockSpec((1, chunk), lambda i: (0, i))
    return pl.pallas_call(
        functools.partial(forcing_kernel, parts),
        grid=(records // chunk,),
        in_specs=[
            pl.BlockSpec(back.shape, lambda i: (0, 0, 0)),
            pl.BlockSpec((chunk, depth), lambda i: (i, 0)),
            row_spec,
            row_spec,
            row_spec,
        ],
        out_specs=pl.BlockSpec((3 * blocks, depth), lambda i: (0, 0)),
        out_shape=jax.ShapeDtypeStruct((3 * blocks, depth), F32),
        scratch_shapes=[pltpu.VMEM((back.shape[0] * 8, 2 * LANES), BF16)],
        compiler_params=pltpu.CompilerParams(dimension_semantics=("arbitrary",)),
        name="forcing",
    )(back, weights, blk, own, slot)


def stream_kernel(
    cur, prev_ref, next_ref, forcing, xu, xd, yu, yd, yu_prev, yu_next, yd_prev, yd_next, corner,
    out_ref,
):
    step = pl.program_id(0)
    last = pl.num_programs(0) - 1
    rows, ny, nz = cur.shape[1:]
    fields = [forcing[c] for c in range(3)]

    def shifted(block, before, after, dx):
        if dx == 1:
            return jnp.concatenate([before[None], block[: rows - 1]], axis=0)
        if dx == -1:
            return jnp.concatenate([block[1:], after[None]], axis=0)
        return block

    for q in range(19):
        dx, dy, dz = lattice_dirs[q]
        before = after = None
        if dx == 1:
            before = jnp.where(step == 0, xu[x_up.index(q)], prev_ref[q, 0])
        if dx == -1:
            after = jnp.where(step == last, xd[x_down.index(q)], next_ref[q, 0])
        moved = shifted(cur[q], before, after, dx)
        if dy != 0:
            k = y_up.index(q) if dy == 1 else y_down.index(q)
            edge = (yu if dy == 1 else yd)[k]
            if dx == 1:
                before = (yu_prev if dy == 1 else yd_prev)[k, 0]
                before = jnp.where(step == 0, corner[diagonal.index(q)], before)
            if dx == -1:
                after = (yu_next if dy == 1 else yd_next)[k, 0]
                after = jnp.where(step == last, corner[diagonal.index(q)], after)
            edge = shifted(edge, before, after, dx)
            turned = pltpu.roll(moved, dy % ny, 1)
            at_edge = iota((rows, ny, nz), 1) == (0 if dy == 1 else ny - 1)
            moved = jnp.where(at_edge, jnp.broadcast_to(edge, (rows, ny, nz)), turned)
        if dz != 0:
            moved = pltpu.roll(moved, dz % nz, 2)
        projected = combine_dirs(fields, lattice_dirs[q])
        if projected is not None:
            moved = moved + (3.0 * lattice_weights[q]) * projected
        out_ref[q] = moved


def stream(relaxed, forcing, xu, xd, yu, yd, corner):
    _, nx, ny, nz = relaxed.shape
    rows = 4
    steps = nx // rows
    before = lambda i: (0, (i * rows + nx - 1) % nx, 0, 0)
    after = lambda i: (0, (i * rows + rows) % nx, 0, 0)
    whole3 = lambda i: (0, 0, 0)
    blocked = lambda i: (0, i, 0, 0)
    return pl.pallas_call(
        stream_kernel,
        grid=(steps,),
        in_specs=[
            pl.BlockSpec((19, rows, ny, nz), blocked),
            pl.BlockSpec((19, 1, ny, nz), before),
            pl.BlockSpec((19, 1, ny, nz), after),
            pl.BlockSpec((3, rows, ny, nz), blocked),
            pl.BlockSpec((5, ny, nz), whole3),
            pl.BlockSpec((5, ny, nz), whole3),
            pl.BlockSpec((5, rows, 1, nz), blocked),
            pl.BlockSpec((5, rows, 1, nz), blocked),
            pl.BlockSpec((5, 1, 1, nz), before),
            pl.BlockSpec((5, 1, 1, nz), after),
            pl.BlockSpec((5, 1, 1, nz), before),
            pl.BlockSpec((5, 1, 1, nz), after),
            pl.BlockSpec((4, 1, nz), whole3),
        ],
        out_specs=pl.BlockSpec((19, rows, ny, nz), blocked),
        out_shape=jax.ShapeDtypeStruct((19, nx, ny, nz), F32),
        compiler_params=pltpu.CompilerParams(dimension_semantics=("arbitrary",)),
        name="stream",
    )(relaxed, relaxed, relaxed, forcing, xu, xd, yu, yd, yu, yu, yd, yd, corner)


def per_device(
    grid, populations, mass, modulus, cell_live, stiff_ref, rec_block, rec_owner, rec_node,
    rbf_weight,
):
    devices = grid[0] * grid[1]
    _, nx, ny, nz = populations.shape
    records = rec_block.shape[0]
    rows, cols = mass.shape
    capacity = 2 * records // devices
    parts = -(-capacity // LANES)
    relaxed, moment, xu, xd, yu, yd = collide(populations)
    blk = rec_block.reshape(1, records)
    own = rec_owner.reshape(1, records)
    node = rec_node.reshape(1, records)
    pay, slot = pack_loads(
        devices, parts, cols, moment.reshape(3 * nx * ny, nz), rbf_weight, blk, own, node
    )
    displacement, back, xu, xd, yu, yd, corner = couple(
        grid, parts, stiff_ref, pay, xu, xd, yu, yd, modulus, cell_live, mass
    )
    forcing = forcing_of(parts, nx * ny, back, rbf_weight, blk, own, slot)
    out = stream(relaxed, forcing.reshape(3, nx, ny, nz), xu, xd, yu, yd, corner)
    return out, displacement


def solution(mesh):
    grid = (mesh.shape["gx"], mesh.shape["gy"])
    in_specs = (
        P(None, "gx", "gy", None),
        P("gx", "gy"),
        P("gx", "gy"),
        P("gx", "gy"),
        P(),
        P(("gx", "gy")),
        P(("gx", "gy"), None),
        P(("gx", "gy")),
        P(("gx", "gy"), None),
    )
    out_specs = (P(None, "gx", "gy", None), P(None, "gx", "gy"))
    return jax.shard_map(
        functools.partial(per_device, grid), mesh=mesh, in_specs=in_specs, out_specs=out_specs,
        check_vma=False,
    )
```

```python
import functools
import math

import jax
import jax.numpy as jnp
from jax import lax
from jax.experimental import pallas as pl
from jax.experimental.pallas import tpu as pltpu
from jax.sharding import PartitionSpec as P

MESH = pl.DeviceIdType.MESH
F32 = jnp.float32
BF16 = jnp.bfloat16
LANES = 128

lattice_dirs = (
    (0, 0, 0),
    (1, 0, 0),
    (-1, 0, 0),
    (0, 1, 0),
    (0, -1, 0),
    (0, 0, 1),
    (0, 0, -1),
    (1, 1, 0),
    (-1, -1, 0),
    (1, -1, 0),
    (-1, 1, 0),
    (1, 0, 1),
    (-1, 0, -1),
    (1, 0, -1),
    (-1, 0, 1),
    (0, 1, 1),
    (0, -1, -1),
    (0, 1, -1),
    (0, -1, 1),
)
lattice_weights = (1.0 / 3.0,) + (1.0 / 18.0,) * 6 + (1.0 / 36.0,) * 12
relax_rate = 1.25
coupling = 0.1

x_up = [q for q in range(19) if lattice_dirs[q][0] == 1]
x_down = [q for q in range(19) if lattice_dirs[q][0] == -1]
y_up = [q for q in range(19) if lattice_dirs[q][1] == 1]
y_down = [q for q in range(19) if lattice_dirs[q][1] == -1]
diagonal = [q for q in range(19) if lattice_dirs[q][0] != 0 and lattice_dirs[q][1] != 0]


def combine_dirs(fields, direction):
    total = None
    for axis_pos in range(3):
        if direction[axis_pos] != 0:
            field = fields[axis_pos]
            if total is None:
                total = field if direction[axis_pos] == 1 else -field
            else:
                total = total + field if direction[axis_pos] == 1 else total - field
    return total


def halves(values):
    high = values.astype(BF16)
    low = (values - high.astype(F32)).astype(BF16)
    return high, low


def iota(shape, dim):
    return lax.broadcasted_iota(jnp.int32, shape, dim)


def dot_nt(left, right):
    return lax.dot_general(left, right, (((1,), (1,)), ((), ())), preferred_element_type=F32)


def dot_nn(left, right):
    return lax.dot_general(left, right, (((1,), (0,)), ((), ())), preferred_element_type=F32)


def collide_kernel(pop_ref, relaxed_ref, moment_ref, xu_ref, xd_ref, yu_ref, yd_ref):
    step = pl.program_id(0)
    last = pl.num_programs(0) - 1
    rows, cols, depth = pop_ref.shape[1:]

    def one(row, carry):
        pops = [pop_ref[q, row] for q in range(19)]
        density = pops[0]
        for q in range(1, 19):
            density = density + pops[q]
        moment = []
        for axis_pos in range(3):
            total = None
            for q in range(19):
                sign = lattice_dirs[q][axis_pos]
                if sign == 1:
                    total = pops[q] if total is None else total + pops[q]
                elif sign == -1:
                    total = -pops[q] if total is None else total - pops[q]
            moment.append(total)
            moment_ref[axis_pos, row] = total
        velocity = [moment[axis_pos] / density for axis_pos in range(3)]
        squared = (
            velocity[0] * velocity[0] + velocity[1] * velocity[1] + velocity[2] * velocity[2]
        )
        rest = 1.0 - 1.5 * squared
        for q in range(19):
            projected = combine_dirs(velocity, lattice_dirs[q])
            bracket = rest
            if projected is not None:
                bracket = rest + projected * (3.0 + 4.5 * projected)
            relaxed = (1.0 - relax_rate) * pops[q] + (
                relax_rate * lattice_weights[q]
            ) * density * bracket
            relaxed_ref[q, row] = relaxed
            if q in y_up:
                yu_ref[y_up.index(q), row] = relaxed[cols - 1 : cols]
            if q in y_down:
                yd_ref[y_down.index(q), row] = relaxed[0:1]
        return carry

    lax.fori_loop(0, rows, one, 0, unroll=2)

    @pl.when(step == 0)
    def _():
        for k, q in enumerate(x_down):
            xd_ref[k] = relaxed_ref[q, 0]

    @pl.when(step == last)
    def _():
        for k, q in enumerate(x_up):
            xu_ref[k] = relaxed_ref[q, rows - 1]


def collide(populations):
    _, nx, ny, nz = populations.shape
    rows = 8
    steps = nx // rows
    return pl.pallas_call(
        collide_kernel,
        grid=(steps,),
        in_specs=[pl.BlockSpec((19, rows, ny, nz), lambda i: (0, i, 0, 0))],
        out_specs=[
            pl.BlockSpec((19, rows, ny, nz), lambda i: (0, i, 0, 0)),
            pl.BlockSpec((3, rows, ny, nz), lambda i: (0, i, 0, 0)),
            pl.BlockSpec((5, ny, nz), lambda i: (0, 0, 0)),
            pl.BlockSpec((5, ny, nz), lambda i: (0, 0, 0)),
            pl.BlockSpec((5, rows, 1, nz), lambda i: (0, i, 0, 0)),
            pl.BlockSpec((5, rows, 1, nz), lambda i: (0, i, 0, 0)),
        ],
        out_shape=[
            jax.ShapeDtypeStruct((19, nx, ny, nz), F32),
            jax.ShapeDtypeStruct((3, nx, ny, nz), F32),
            jax.ShapeDtypeStruct((5, ny, nz), F32),
            jax.ShapeDtypeStruct((5, ny, nz), F32),
            jax.ShapeDtypeStruct((5, nx, 1, nz), F32),
            jax.ShapeDtypeStruct((5, nx, 1, nz), F32),
        ],
        compiler_params=pltpu.CompilerParams(dimension_semantics=("arbitrary",)),
        name="collide",
    )(populations)


def pack_kernel(
    devices, parts, node_cols, mom_ref, w_ref, blk_ref, own_ref, node_ref,
    out_ref, slot_ref, mom_cat, tri, base, acc,
):
    step = pl.program_id(0)
    blocks = mom_ref.shape[0] // 3
    chunk = w_ref.shape[0]

    @pl.when(step == 0)
    def _():
        high, low = halves(mom_ref[...])
        mom_cat[...] = jnp.concatenate([high, low, high], axis=1)
        before = iota((chunk, chunk), 0) <= iota((chunk, chunk), 1)
        tri[...] = before.astype(F32).astype(BF16)
        base[...] = jnp.zeros_like(base)
        acc[...] = jnp.zeros_like(acc)

    w_high, w_low = halves(w_ref[...])
    products = dot_nt(mom_cat[...], jnp.concatenate([w_high, w_high, w_low], axis=1))
    here = iota((blocks, chunk), 0) == blk_ref[...]
    loads = [
        jnp.sum(
            jnp.where(here, products[c * blocks : (c + 1) * blocks], 0.0), axis=0, keepdims=True
        )
        for c in range(3)
    ]
    owners = own_ref[...]
    hits = (iota((devices, chunk), 0) == owners).astype(F32)
    counts = dot_nn(hits.astype(BF16), tri[...])
    slots = jnp.sum(hits * (counts - 1.0 + base[:, 0:1]), axis=0, keepdims=True)
    base[...] = base[...] + counts[:, chunk - 1 : chunk]
    slot_id = slots.astype(jnp.int32)
    slot_ref[...] = slot_id
    part = slot_id // LANES
    place = slot_id - part * LANES
    node = node_ref[...]
    node_row = node // node_cols
    node_high = (node_row * node_cols).astype(F32)
    node_low = (node - node_row * node_cols).astype(F32)
    channel = iota((8, chunk), 0) // parts
    in_part = (iota((8, chunk), 0) - channel * parts) == part
    high_rows = jnp.zeros((8, chunk), F32)
    low_rows = jnp.zeros((8, chunk), F32)
    for c in range(4):
        if c < 3:
            high = loads[c].astype(BF16).astype(F32)
            low = loads[c] - high
        else:
            high, low = node_high, node_low
        high_rows = jnp.where(in_part & (channel == c), high, high_rows)
        low_rows = jnp.where(in_part & (channel == c), low, low_rows)
    mine = (iota((devices * 8, chunk), 0) // 8) == owners

    def spread(rows):
        tiled = jnp.broadcast_to(rows[None], (devices, 8, chunk)).reshape(devices * 8, chunk)
        return jnp.where(mine, tiled, 0.0).astype(BF16)

    slot_hot = (iota((LANES, chunk), 0) == place).astype(F32).astype(BF16)
    acc[...] += dot_nt(
        jnp.concatenate([spread(high_rows), spread(low_rows)], axis=1),
        jnp.concatenate([slot_hot, slot_hot], axis=1),
    )

    @pl.when(step == pl.num_programs(0) - 1)
    def _():
        out_ref[...] = acc[...].reshape(devices, 8, LANES)


def pack_loads(devices, parts, node_cols, moment, weights, blk, own, node):
    records, depth = weights.shape
    chunk = 512
    rows3 = moment.shape[0]
    row_spec = pl.BlockSpec((1, chunk), lambda i: (0, i))
    return pl.pallas_call(
        functools.partial(pack_kernel, devices, parts, node_cols),
        grid=(records // chunk,),
        in_specs=[
            pl.BlockSpec((rows3, depth), lambda i: (0, 0)),
            pl.BlockSpec((chunk, depth), lambda i: (i, 0)),
            row_spec,
            row_spec,
            row_spec,
        ],
        out_specs=[
            pl.BlockSpec((devices, 8, LANES), lambda i: (0, 0, 0)),
            row_spec,
        ],
        out_shape=[
            jax.ShapeDtypeStruct((devices, 8, LANES), F32),
            jax.ShapeDtypeStruct((1, records), jnp.int32),
        ],
        scratch_shapes=[
            pltpu.VMEM((rows3, 3 * depth), BF16),
            pltpu.VMEM((chunk, chunk), BF16),
            pltpu.VMEM((devices, LANES), F32),
            pltpu.VMEM((devices * 8, LANES), F32),
        ],
        compiler_params=pltpu.CompilerParams(dimension_semantics=("arbitrary",)),
        name="pack_loads",
    )(moment, weights, blk, own, node)


def position(grid):
    return lax.axis_index("gx"), lax.axis_index("gy")


def greet_all(grid):
    ix, iy = position(grid)
    devices = grid[0] * grid[1]
    me = ix * grid[1] + iy
    barrier = pltpu.get_barrier_semaphore()

    def signal(j, carry):
        other = lax.rem(me + j, devices)
        pl.semaphore_signal(
            barrier, inc=1, device_id=(lax.div(other, grid[1]), lax.rem(other, grid[1])),
            device_id_type=MESH,
        )
        return carry

    lax.fori_loop(1, devices, signal, 0)
    pl.semaphore_wait(barrier, devices - 1)


def broadcast_copy(grid, j, source, target, send_sem, recv_sem):
    ix, iy = position(grid)
    devices = grid[0] * grid[1]
    me = ix * grid[1] + iy
    other = lax.rem(me + j, devices)
    return pltpu.make_async_remote_copy(
        src_ref=source(other),
        dst_ref=target(me),
        send_sem=send_sem.at[j],
        recv_sem=recv_sem.at[j],
        device_id=(lax.div(other, grid[1]), lax.rem(other, grid[1])),
        device_id_type=MESH,
    )


def to_all(grid, source, target, send_sem, recv_sem, start):
    def body(j, carry):
        copy = broadcast_copy(grid, j, source, target, send_sem, recv_sem)
        if start:
            copy.start()
        else:
            copy.wait()
        return carry

    lax.fori_loop(1, grid[0] * grid[1], body, 0)


def neighbour_copy(grid, dx, dy, source, target, send_sem, recv_sem):
    ix, iy = position(grid)
    return pltpu.make_async_remote_copy(
        src_ref=source,
        dst_ref=target,
        send_sem=send_sem,
        recv_sem=recv_sem,
        device_id=(lax.rem(ix + dx + grid[0], grid[0]), lax.rem(iy + dy + grid[1], grid[1])),
        device_id_type=MESH,
    )


def rim_copies(grid, field, side, strip, send_sem, recv_sem):
    rows = field.shape[1]
    copies = [
        neighbour_copy(grid, 0, 1, field, side.at[0], send_sem.at[0], recv_sem.at[0]),
        neighbour_copy(grid, 0, -1, field, side.at[1], send_sem.at[1], recv_sem.at[1]),
    ]
    for k in range(3):
        dy = 1 - k
        copies.append(
            neighbour_copy(
                grid, 1, dy, field.at[:, pl.ds(rows - 8, 8), :], strip.at[k],
                send_sem.at[2 + k], recv_sem.at[2 + k],
            )
        )
    for k in range(3):
        dy = 1 - k
        copies.append(
            neighbour_copy(
                grid, -1, dy, field.at[:, pl.ds(0, 8), :], strip.at[3 + k],
                send_sem.at[5 + k], recv_sem.at[5 + k],
            )
        )
    return copies


def lines_of(ref, first, count, row, parts):
    return jnp.concatenate(
        [ref[first + d, row + p : row + p + 1] for d in range(count) for p in range(parts)],
        axis=1,
    )


def node_hots(ref, first, count, parts, rows, cols):
    node = lines_of(ref, first, count, 3 * parts, parts).astype(jnp.int32)
    row = node // cols
    col = node - row * cols
    width = count * parts * LANES
    row_hot = iota((rows, width), 0) == row
    col_hot = (iota((cols, width), 0) == col).astype(F32).astype(BF16)
    return row_hot, col_hot


def gather_force(parts, pay, force):
    devices = pay.shape[0]
    rows, cols = force.shape[1:]
    count = math.gcd(devices, 4)

    def one(step, total):
        first = step * count
        row_hot, col_hot = node_hots(pay, first, count, parts, rows, cols)
        highs = []
        lows = []
        for c in range(3):
            value = lines_of(pay, first, count, c * parts, parts)
            high = value.astype(BF16).astype(F32)
            highs.append(jnp.where(row_hot, high, 0.0).astype(BF16))
            lows.append(jnp.where(row_hot, value - high, 0.0).astype(BF16))
        left = jnp.concatenate(
            [jnp.concatenate(highs, axis=0), jnp.concatenate(lows, axis=0)], axis=1
        )
        return total + dot_nt(left, jnp.concatenate([col_hot, col_hot], axis=1))

    total = lax.fori_loop(0, devices // count, one, jnp.zeros((3 * rows, cols), F32))
    for c in range(3):
        force[c] = total[c * rows : (c + 1) * rows]


def pick_moved(parts, disp, pay, out):
    devices = pay.shape[0]
    rows, cols = disp[0].shape
    count = math.gcd(devices, 4)
    high, low = halves(jnp.concatenate(disp, axis=0))
    left = jnp.concatenate([high, low], axis=1)

    def one(step, carry):
        first = step * count
        row_hot, col_hot = node_hots(pay, first, count, parts, rows, cols)
        found = dot_nn(left, jnp.concatenate([col_hot, col_hot], axis=0))
        values = [
            jnp.sum(
                jnp.where(row_hot, found[c * rows : (c + 1) * rows], 0.0), axis=0, keepdims=True
            )
            for c in range(3)
        ]
        for d in range(count):
            pieces = []
            for value in values:
                for p in range(parts):
                    at = (d * parts + p) * LANES
                    pieces.append(value[:, at : at + LANES])
            pieces.append(jnp.zeros((8 - 3 * parts, LANES), F32))
            out[first + d] = jnp.concatenate(pieces, axis=0)
        return carry

    lax.fori_loop(0, devices // count, one, 0)


def with_rim(centre, side, strip, c):
    rows, cols = centre.shape[1:]
    left_half = iota((rows, cols), 1) < cols // 2
    main = jnp.concatenate([centre[c], jnp.where(left_half, side[1, c], side[0, c])], axis=1)
    low = iota((8, cols), 0) < 4
    left_strip = iota((8, cols), 1) < cols // 2
    below = jnp.where(low, strip[4, c], strip[1, c])
    corner = jnp.where(
        low,
        jnp.where(left_strip, strip[5, c], strip[3, c]),
        jnp.where(left_strip, strip[2, c], strip[0, c]),
    )
    return jnp.concatenate([main, jnp.concatenate([below, corner], axis=1)], axis=0)


def couple_kernel(
    grid, parts, stiff, pay, xu, xd, yu, yd, modulus_ref, live_ref, mass_ref,
    disp, back_in, xu_in, xd_in, yu_in, yd_in, corner_in,
    pay_in, back, stat, stat_side, stat_strip, force, side, strip, one_buf, two_buf,
    pay_send, pay_recv, back_send, back_recv, lb_send, lb_recv,
    stat_send, stat_recv, rim_send, rim_recv, one_send, one_recv, two_send, two_recv,
):
    ix, iy = position(grid)
    me = ix * grid[1] + iy
    rows, cols = force.shape[1:]
    full = (rows + 8, 2 * cols)
    stat[0] = modulus_ref[...]
    stat[1] = live_ref[...].astype(F32)
    stat[2] = mass_ref[...]
    greet_all(grid)
    to_all(grid, lambda o: pay.at[o], lambda m: pay_in.at[m], pay_send, pay_recv, True)
    stat_copies = rim_copies(grid, stat, stat_side, stat_strip, stat_send, stat_recv)
    nx = yu.shape[1]
    plan = [
        (1, 0, xu, xu_in),
        (-1, 0, xd, xd_in),
        (0, 1, yu, yu_in),
        (0, -1, yd, yd_in),
    ]
    for k, q in enumerate(diagonal):
        dx, dy, _ = lattice_dirs[q]
        edge = yu.at[y_up.index(q)] if dy == 1 else yd.at[y_down.index(q)]
        plan.append((dx, dy, edge.at[nx - 1 if dx == 1 else 0], corner_in.at[k]))
    lb_copies = [
        neighbour_copy(grid, dx, dy, source, target, lb_send.at[number], lb_recv.at[number])
        for number, (dx, dy, source, target) in enumerate(plan)
    ]
    pay_in[me] = pay[me]
    to_all(grid, lambda o: pay.at[o], lambda m: pay_in.at[m], pay_send, pay_recv, False)
    for copy in stat_copies + lb_copies:
        copy.start()
    gather_force(parts, pay_in, force)
    copies = rim_copies(grid, force, side, strip, rim_send, rim_recv)
    for copy in copies:
        copy.start()

    def back_row(a):
        return pltpu.roll(a, full[0] - 1, 0)

    def back_col(a):
        return pltpu.roll(a, full[1] - 1, 1)

    for copy in stat_copies:
        copy.wait()
    moduli = with_rim(stat, stat_side, stat_strip, 0)
    live = with_rim(stat, stat_side, stat_strip, 1)
    mass = with_rim(stat, stat_side, stat_strip, 2)
    next_row = back_row(moduli)
    scale = live * (moduli + next_row + back_col(moduli) + back_col(next_row)) * 0.25

    def operate(fields):
        down = [back_row(f) for f in fields]
        corners = (
            list(fields) + down + [back_col(f) for f in fields] + [back_col(f) for f in down]
        )
        results = []
        for k in range(12):
            total = stiff[k, 0] * corners[0]
            for l in range(1, 12):
                total = total + stiff[k, l] * corners[l]
            results.append(scale * total)
        images = []
        for c in range(3):
            right = results[6 + c] + pltpu.roll(results[9 + c], 1, 0)
            images.append(
                mass * fields[c]
                + results[c]
                + pltpu.roll(results[3 + c], 1, 0)
                + pltpu.roll(right, 1, 1)
            )
        return images

    def inner(a, b):
        total = a[0][:rows, :cols] * b[0][:rows, :cols]
        for c in range(1, 3):
            total = total + a[c][:rows, :cols] * b[c][:rows, :cols]
        return jnp.sum(jnp.sum(total, axis=0, keepdims=True), axis=1, keepdims=True)

    def sum_over_devices(values, buf, send_sem, recv_sem):
        lane = iota((1, LANES), 1)
        line = jnp.zeros((1, LANES), F32)
        for k, value in enumerate(values):
            line = jnp.where(lane == k, value, line)
        buf[me] = line
        source = lambda o: buf.at[me]
        target = lambda m: buf.at[m]
        to_all(grid, source, target, send_sem, recv_sem, True)
        to_all(grid, source, target, send_sem, recv_sem, False)
        total = jnp.sum(buf[...], axis=0)
        return [total[:, k : k + 1] for k in range(len(values))]

    for copy in copies:
        copy.wait()
    field = [with_rim(force, side, strip, c) for c in range(3)]
    image = operate(field)
    ff, fq = sum_over_devices(
        [inner(field, field), inner(field, image)], one_buf, one_send, one_recv
    )
    first = ff / fq
    residual = [field[c] - first * image[c] for c in range(3)]
    second_image = operate(residual)
    rr, rs, rq = sum_over_devices(
        [inner(residual, residual), inner(residual, second_image), inner(residual, image)],
        two_buf, two_send, two_recv,
    )
    ratio = rr / ff
    second = rr / (rs + 2.0 * ratio * rq + ratio * ratio * fq)
    moved = []
    for c in range(3):
        f = field[c][:rows, :cols]
        moved.append(first * f + second * (residual[c][:rows, :cols] + ratio * f))
        disp[c] = moved[c]
    pick_moved(parts, moved, pay_in, back)
    to_all(grid, lambda o: back.at[o], lambda m: back_in.at[m], back_send, back_recv, True)
    back_in[me] = back[me]
    to_all(grid, lambda o: back.at[o], lambda m: back_in.at[m], back_send, back_recv, False)
    for copy in lb_copies:
        copy.wait()


def couple(grid, parts, stiff, pay, xu, xd, yu, yd, modulus, live, mass):
    devices = grid[0] * grid[1]
    depth = xu.shape[2]
    patch = (3,) + mass.shape
    shapes = [patch, pay.shape, xu.shape, xd.shape, yu.shape, yd.shape, (4, 1, depth)]
    vmem = pl.BlockSpec(memory_space=pltpu.VMEM)
    rim = [pltpu.VMEM((2,) + patch, F32), pltpu.VMEM((6, 3, 8, patch[2]), F32)]
    to_each = pltpu.SemaphoreType.DMA((devices,))
    to_near = pltpu.SemaphoreType.DMA((8,))
    return pl.pallas_call(
        functools.partial(couple_kernel, grid, parts),
        in_specs=[pl.BlockSpec(memory_space=pltpu.SMEM)] + [vmem] * 8,
        out_specs=[vmem] * len(shapes),
        out_shape=[jax.ShapeDtypeStruct(shape, F32) for shape in shapes],
        scratch_shapes=[
            pltpu.VMEM(pay.shape, F32),
            pltpu.VMEM(pay.shape, F32),
            pltpu.VMEM(patch, F32),
            *rim,
            pltpu.VMEM(patch, F32),
            *rim,
            pltpu.VMEM((devices, 1, LANES), F32),
            pltpu.VMEM((devices, 1, LANES), F32),
            to_each, to_each, to_each, to_each, to_near, to_near,
            to_near, to_near, to_near, to_near, to_each, to_each, to_each, to_each,
        ],
        compiler_params=pltpu.CompilerParams(collective_id=0, has_side_effects=True),
        name="couple",
    )(stiff, pay, xu, xd, yu, yd, modulus, live, mass)


def forcing_kernel(parts, back_ref, w_ref, blk_ref, own_ref, slot_ref, out_ref, back_cat):
    step = pl.program_id(0)
    devices = back_ref.shape[0]
    blocks = out_ref.shape[0] // 3
    chunk = w_ref.shape[0]

    @pl.when(step == 0)
    def _():
        high, low = halves(back_ref[...].reshape(devices * 8, LANES))
        back_cat[...] = jnp.concatenate([high, low], axis=1)
        out_ref[...] = jnp.zeros_like(out_ref)

    slot_id = slot_ref[...]
    part = slot_id // LANES
    place = slot_id - part * LANES
    slot_hot = (iota((LANES, chunk), 0) == place).astype(F32).astype(BF16)
    found = dot_nn(back_cat[...], jnp.concatenate([slot_hot, slot_hot], axis=0))
    mine = (iota((devices * 8, chunk), 0) // 8) == own_ref[...]
    lines = jnp.sum(jnp.where(mine, found, 0.0).reshape(devices, 8, chunk), axis=0)
    channel = iota((8, chunk), 0) // parts
    in_part = (iota((8, chunk), 0) - channel * parts) == part
    here = iota((blocks, chunk), 0) == blk_ref[...]
    highs = []
    lows = []
    for c in range(3):
        moved = coupling * jnp.sum(
            jnp.where(in_part & (channel == c), lines, 0.0), axis=0, keepdims=True
        )
        high = moved.astype(BF16).astype(F32)
        highs.append(jnp.where(here, high, 0.0).astype(BF16))
        lows.append(jnp.where(here, moved - high, 0.0).astype(BF16))
    high = jnp.concatenate(highs, axis=0)
    low = jnp.concatenate(lows, axis=0)
    w_high, w_low = halves(w_ref[...])
    out_ref[...] += dot_nn(
        jnp.concatenate([high, low, high], axis=1),
        jnp.concatenate([w_high, w_high, w_low], axis=0),
    )


def forcing_of(parts, blocks, back, weights, blk, own, slot):
    records, depth = weights.shape
    chunk = 1024
    row_spec = pl.BlockSpec((1, chunk), lambda i: (0, i))
    return pl.pallas_call(
        functools.partial(forcing_kernel, parts),
        grid=(records // chunk,),
        in_specs=[
            pl.BlockSpec(back.shape, lambda i: (0, 0, 0)),
            pl.BlockSpec((chunk, depth), lambda i: (i, 0)),
            row_spec,
            row_spec,
            row_spec,
        ],
        out_specs=pl.BlockSpec((3 * blocks, depth), lambda i: (0, 0)),
        out_shape=jax.ShapeDtypeStruct((3 * blocks, depth), F32),
        scratch_shapes=[pltpu.VMEM((back.shape[0] * 8, 2 * LANES), BF16)],
        compiler_params=pltpu.CompilerParams(dimension_semantics=("arbitrary",)),
        name="forcing",
    )(back, weights, blk, own, slot)


def stream_kernel(
    cur, prev_ref, next_ref, forcing, xu, xd, yu, yd, yu_prev, yu_next, yd_prev, yd_next, corner,
    out_ref,
):
    step = pl.program_id(0)
    last = pl.num_programs(0) - 1
    rows, ny, nz = cur.shape[1:]
    fields = [forcing[c] for c in range(3)]

    def shifted(block, before, after, dx):
        if dx == 1:
            return jnp.concatenate([before[None], block[: rows - 1]], axis=0)
        if dx == -1:
            return jnp.concatenate([block[1:], after[None]], axis=0)
        return block

    for q in range(19):
        dx, dy, dz = lattice_dirs[q]
        before = after = None
        if dx == 1:
            before = jnp.where(step == 0, xu[x_up.index(q)], prev_ref[q, 0])
        if dx == -1:
            after = jnp.where(step == last, xd[x_down.index(q)], next_ref[q, 0])
        moved = shifted(cur[q], before, after, dx)
        if dy != 0:
            k = y_up.index(q) if dy == 1 else y_down.index(q)
            edge = (yu if dy == 1 else yd)[k]
            if dx == 1:
                before = (yu_prev if dy == 1 else yd_prev)[k, 0]
                before = jnp.where(step == 0, corner[diagonal.index(q)], before)
            if dx == -1:
                after = (yu_next if dy == 1 else yd_next)[k, 0]
                after = jnp.where(step == last, corner[diagonal.index(q)], after)
            edge = shifted(edge, before, after, dx)
            turned = pltpu.roll(moved, dy % ny, 1)
            at_edge = iota((rows, ny, nz), 1) == (0 if dy == 1 else ny - 1)
            moved = jnp.where(at_edge, jnp.broadcast_to(edge, (rows, ny, nz)), turned)
        if dz != 0:
            moved = pltpu.roll(moved, dz % nz, 2)
        projected = combine_dirs(fields, lattice_dirs[q])
        if projected is not None:
            moved = moved + (3.0 * lattice_weights[q]) * projected
        out_ref[q] = moved


def stream(relaxed, forcing, xu, xd, yu, yd, corner):
    _, nx, ny, nz = relaxed.shape
    rows = 8
    steps = nx // rows
    before = lambda i: (0, (i * rows + nx - 1) % nx, 0, 0)
    after = lambda i: (0, (i * rows + rows) % nx, 0, 0)
    whole3 = lambda i: (0, 0, 0)
    blocked = lambda i: (0, i, 0, 0)
    return pl.pallas_call(
        stream_kernel,
        grid=(steps,),
        in_specs=[
            pl.BlockSpec((19, rows, ny, nz), blocked),
            pl.BlockSpec((19, 1, ny, nz), before),
            pl.BlockSpec((19, 1, ny, nz), after),
            pl.BlockSpec((3, rows, ny, nz), blocked),
            pl.BlockSpec((5, ny, nz), whole3),
            pl.BlockSpec((5, ny, nz), whole3),
            pl.BlockSpec((5, rows, 1, nz), blocked),
            pl.BlockSpec((5, rows, 1, nz), blocked),
            pl.BlockSpec((5, 1, 1, nz), before),
            pl.BlockSpec((5, 1, 1, nz), after),
            pl.BlockSpec((5, 1, 1, nz), before),
            pl.BlockSpec((5, 1, 1, nz), after),
            pl.BlockSpec((4, 1, nz), whole3),
        ],
        out_specs=pl.BlockSpec((19, rows, ny, nz), blocked),
        out_shape=jax.ShapeDtypeStruct((19, nx, ny, nz), F32),
        compiler_params=pltpu.CompilerParams(dimension_semantics=("arbitrary",)),
        name="stream",
    )(relaxed, relaxed, relaxed, forcing, xu, xd, yu, yd, yu, yu, yd, yd, corner)


def per_device(
    grid, populations, mass, modulus, cell_live, stiff_ref, rec_block, rec_owner, rec_node,
    rbf_weight,
):
    devices = grid[0] * grid[1]
    _, nx, ny, nz = populations.shape
    records = rec_block.shape[0]
    rows, cols = mass.shape
    capacity = 2 * records // devices
    parts = -(-capacity // LANES)
    relaxed, moment, xu, xd, yu, yd = collide(populations)
    blk = rec_block.reshape(1, records)
    own = rec_owner.reshape(1, records)
    node = rec_node.reshape(1, records)
    pay, slot = pack_loads(
        devices, parts, cols, moment.reshape(3 * nx * ny, nz), rbf_weight, blk, own, node
    )
    displacement, back, xu, xd, yu, yd, corner = couple(
        grid, parts, stiff_ref, pay, xu, xd, yu, yd, modulus, cell_live, mass
    )
    forcing = forcing_of(parts, nx * ny, back, rbf_weight, blk, own, slot)
    out = stream(relaxed, forcing.reshape(3, nx, ny, nz), xu, xd, yu, yd, corner)
    return out, displacement


def solution(mesh):
    grid = (mesh.shape["gx"], mesh.shape["gy"])
    in_specs = (
        P(None, "gx", "gy", None),
        P("gx", "gy"),
        P("gx", "gy"),
        P("gx", "gy"),
        P(),
        P(("gx", "gy")),
        P(("gx", "gy"), None),
        P(("gx", "gy")),
        P(("gx", "gy"), None),
    )
    out_specs = (P(None, "gx", "gy", None), P(None, "gx", "gy"))
    return jax.shard_map(
        functools.partial(per_device, grid), mesh=mesh, in_specs=in_specs, out_specs=out_specs,
        check_vma=False,
    )
```
